32 devices in a mesh: vtx: 8 (over y, x, core), edg: 4 (over z).
Axes of the slice: x: 2, y: 2, z: 4, core: 2. Of those that a mesh axis runs over, the one named last changes fastest.
Arguments:
- sketch_cols: bfloat16 [131072, 128], P(('vtx', 'edg')), may hold values from -6 to 6
- edge_weight: float32 [131072], P(('vtx', 'edg')), may hold values from 0.25 to 4
- ground: float32 [16384], P('vtx'), may hold values from 0.05 to 0.5
- src_local: int32 [131072], P(('vtx', 'edg')), may hold values from 0 to 2047
- dst_index: int32 [131072], P(('vtx', 'edg')), may hold values from 0 to 2431
- send_rows: int32 [32, 8, 48], P(('vtx', 'edg')), may hold values from 0 to 2047
- edge_count: int32 [32], P(('vtx', 'edg')), may hold values from 512 to 4096, as said below
Outputs:
- solution: float32 [16384, 128], P('vtx')
- resistance: float32 [131072], P(('vtx', 'edg'))
The draws below stay inside these ranges and needn't reach their ends.
Inputs may be any that keep to these rules, and one draw needn't show every extreme that they name: `edge_count`: edge slots of a device at positions of its count or beyond are unused. In every draw some device has all 4096 slots live.
All inputs are finite; a program needn't handle non-finite values.
Results may differ from the reference program's by a relative error of at most 0.0003.
Values sent between devices are 32-bit elements; how exact they have to be, the bound alone decides.
A program may use at most 64 MiB of HBM per device.

```python
import math
import jax
import jax.numpy as jnp
from jax import lax

COLS = 128
VB = 2048
ED = 4096
H = 48
ITERS = 3
GROUPS = 32
V = 16384
EDGES = 131072
N_VTX = 8
N_EDG = 4


def draw_edge_count(key, part):
    mixed = jax.random.fold_in(key, 11)
    first_key, second_key = jax.random.split(mixed)
    powers = jax.random.randint(first_key, (GROUPS,), 0, 4)
    counts = jnp.right_shift(jnp.full((GROUPS,), ED, jnp.int32), powers.astype(jnp.int32))
    chosen = jax.random.randint(second_key, (), 0, GROUPS)
    counts = counts.at[chosen].set(ED)
    return counts.astype(jnp.int32)


def set_ends(array, rng, smallest, high):
    dims = array.shape
    index_at = [jax.random.randint(jax.random.fold_in(rng, axis), (), 0, dims[axis]) for axis in range(len(dims))]
    array = array.at[tuple(index_at)].set(smallest)
    longest = dims.index(max(dims))
    index_at[longest] = (index_at[longest] + 1) % dims[longest]
    return array.at[tuple(index_at)].set(high)


def level_of(own_key, shape, pieces, low, top_value):
    gain = 1.0
    for axis_at, parts in pieces:
        steps = jax.random.uniform(jax.random.fold_in(jax.random.fold_in(own_key, 6), axis_at), (parts,), jnp.float32, low / len(pieces), top_value / len(pieces))
        gain = gain * jnp.repeat(jnp.exp(steps), shape[axis_at] // parts).reshape((-1,) + (1,) * (len(shape) - 1 - axis_at))
    return gain


def gaussian(own_key, extent, deviation, reach, cuts=(), kind=jnp.bfloat16):
    entries = jax.random.normal(own_key, extent, jnp.float32) * deviation
    if len(cuts) > 0:
        entries = level_of(own_key, extent, cuts, -0.22, 0.18) * entries
    return jnp.clip(entries, min=-reach, max=reach).astype(kind)


def setup_inputs(seed: int = 0) -> dict:
    streams_of = jax.random.split(jax.random.key(seed), 8)
    sketch_cols = gaussian(streams_of[0], (EDGES, COLS), 1.0, 6.0, ((0, 32),))
    edge_weight = jnp.clip(jnp.exp(math.log(4.0) - 2.7725887 * jax.random.uniform(streams_of[1], (EDGES,), jnp.float32) ** level_of(streams_of[1], (EDGES,), ((0, 32),), -0.2, 0.2)), 0.25, 4.0)
    ground = jnp.clip(jnp.exp(math.log(0.5) - 2.3025851 * jax.random.uniform(streams_of[2], (V,), jnp.float32) ** level_of(streams_of[2], (V,), ((0, 8),), -0.2, 0.2)), 0.05, 0.5)
    src_local = set_ends(jax.random.randint(streams_of[3], (EDGES,), 0, VB), jax.random.fold_in(streams_of[3], 1), 0, VB - 1).astype(jnp.int32)
    dst_index = set_ends(jax.random.randint(streams_of[4], (EDGES,), 0, VB + N_VTX * H), jax.random.fold_in(streams_of[4], 1), 0, (VB + N_VTX * H) - 1).astype(jnp.int32)
    send_rows = set_ends(jax.random.randint(streams_of[5], (GROUPS, N_VTX, H), 0, VB), jax.random.fold_in(streams_of[5], 1), 0, VB - 1).astype(jnp.int32)
    edge_count = draw_edge_count(jax.random.fold_in(streams_of[7], 71), 0)
    return {"sketch_cols": sketch_cols, "edge_weight": edge_weight, "ground": ground, "src_local": src_local, "dst_index": dst_index, "send_rows": send_rows, "edge_count": edge_count}


lam_low = 0.05
lam_high = 2.0

def chebyshev_terms(steps):
    centre = (lam_high + lam_low) / 2.0
    half_width = (lam_high - lam_low) / 2.0
    sigma_val = centre / half_width
    rho_prev = 1.0 / sigma_val
    pairs = []
    for count_idx in range(steps - 1):
        rho_next = 1.0 / (2.0 * sigma_val - rho_prev)
        pairs.append((rho_next * rho_prev, 2.0 * rho_next / half_width))
        rho_prev = rho_next
    return (1.0 / centre, pairs)

def reference(sketch_cols, edge_weight, ground, src_local, dst_index, send_rows, edge_count):
    vertices = VB * N_VTX
    position = jnp.arange(EDGES, dtype=jnp.int32)
    device = position // ED
    block_id = device // N_EDG
    lane_idx = device % N_EDG
    live_mask = (position % ED < edge_count[device]).astype(jnp.float32)
    source = block_id * VB + src_local
    slot_idx = jnp.maximum(dst_index - VB, 0)
    owner_blk = slot_idx // H
    within = slot_idx % H
    remote = send_rows[owner_blk * N_EDG + lane_idx, block_id, within]
    target = jnp.where(dst_index < VB, block_id * VB + dst_index, owner_blk * VB + remote).astype(jnp.int32)
    weight_live = edge_weight * live_mask
    root_live = jnp.sqrt(edge_weight) * live_mask
    edge_terms = root_live[:, None] * sketch_cols.astype(jnp.float32)
    right_side = jax.ops.segment_sum(edge_terms, source, vertices) - jax.ops.segment_sum(edge_terms, target, vertices)
    degree = jax.ops.segment_sum(weight_live, source, vertices) + jax.ops.segment_sum(weight_live, target, vertices)
    inverse = (1.0 / (degree + ground))[:, None]

    def operate(field_in):
        edge_diffs = weight_live[:, None] * (field_in[source] - field_in[target])
        return ground[:, None] * field_in + jax.ops.segment_sum(edge_diffs, source, vertices) - jax.ops.segment_sum(edge_diffs, target, vertices)
    first, pairs = chebyshev_terms(ITERS)
    residual_now = right_side
    direction = first * inverse * right_side
    solution = jnp.zeros_like(right_side)
    for step_idx in range(ITERS):
        solution = solution + direction
        if step_idx + 1 < ITERS:
            residual_now = residual_now - operate(direction)
            keep_coef, push_coef = pairs[step_idx]
            direction = keep_coef * direction + push_coef * inverse * residual_now
    gaps = solution[source] - solution[target]
    resistance = live_mask * lax.optimization_barrier(jnp.sum(gaps * gaps, axis=1)) / COLS
    return (solution, resistance)
```

```python
import functools

import jax
import jax.numpy as jnp
from jax import lax
from jax.experimental import pallas as pl
from jax.experimental.pallas import tpu as pltpu
from jax.sharding import PartitionSpec as P

ITERS = 3

lam_low = 0.05
lam_high = 2.0
LANES = 128
VMEM_LIMIT = 62 * 1024 * 1024
GROUP = 512
PIECE = 128
LAG = 3


def chebyshev_terms(steps):
    centre = (lam_high + lam_low) / 2.0
    half_width = (lam_high - lam_low) / 2.0
    sigma_val = centre / half_width
    rho_prev = 1.0 / sigma_val
    pairs = []
    for count_idx in range(steps - 1):
        rho_next = 1.0 / (2.0 * sigma_val - rho_prev)
        pairs.append((rho_next * rho_prev, 2.0 * rho_next / half_width))
        rho_prev = rho_next
    return (1.0 / centre, pairs)


def split2(x):
    hi = x.astype(jnp.bfloat16)
    lo = (x - hi.astype(jnp.float32)).astype(jnp.bfloat16)
    return hi, lo


def split3(x):
    hi = x.astype(jnp.bfloat16)
    rest = x - hi.astype(jnp.float32)
    mid, lo = split2(rest)
    return hi, mid, lo


def pair(x):
    return jnp.concatenate(split2(x), axis=1)


def halves(x):
    n = x.shape[1] // 2
    return x[:, :n] + x[:, n:]


def dot(a, b):
    return jnp.dot(a, b, preferred_element_type=jnp.float32)


def signed(is_src, is_dst):
    one, none = jnp.ones(is_src.shape, jnp.bfloat16), jnp.zeros(is_src.shape, jnp.bfloat16)
    return jnp.where(is_src, one, jnp.where(is_dst, -one, none))


def one_hot(match):
    return jnp.where(match, jnp.ones(match.shape, jnp.bfloat16), jnp.zeros(match.shape, jnp.bfloat16))


def short(x, shape):
    return jnp.broadcast_to(jnp.asarray(x, jnp.int32), shape).astype(jnp.int16)


def down_rows(row, at, rows):
    shape = (rows, row.shape[1])
    return lax.broadcasted_iota(jnp.int16, shape, 0) == jnp.broadcast_to((row - at).astype(jnp.int16), shape)


def along_lanes(spread, at, width):
    parts = []
    lane = lax.broadcasted_iota(jnp.int16, spread.shape, 1)
    for off in range(0, width, LANES):
        parts.append(lane + short(at + off, spread.shape) == spread)
    return parts


def even_piece(total, most):
    return max(n for n in range(8, most + 1, 8) if total % n == 0)


def remote(src, dst, send_sem, recv_sem, target):
    return pltpu.make_async_remote_copy(
        src_ref=src, dst_ref=dst, send_sem=send_sem, recv_sem=recv_sem,
        device_id=target, device_id_type=pl.DeviceIdType.MESH,
    )


def exchange(me, peers, src, dst, send_sem, recv_sem):
    def start(off, _):
        to = lax.rem(me + off, peers)
        remote(src(to), dst.at[me], send_sem.at[off], recv_sem.at[off], {"vtx": to}).start()
        return 0

    lax.fori_loop(1, peers, start, 0)


def exchange_wait(me, peers, src, dst, send_sem, recv_sem):
    def wait(off, _):
        to = lax.rem(me + off, peers)
        origin = lax.rem(me + peers - off, peers)
        remote(src(to), dst.at[origin], send_sem.at[off], recv_sem.at[off], {"vtx": to}).wait()
        return 0

    lax.fori_loop(1, peers, wait, 0)


def kernel(
    peers, sketch_ref, weight_ref, ground_ref, src_ref, dst_ref, list_ref, count_ref, sol_ref, gap_ref,
    rowf, srow, dstb, wide, wb, listb, listrow, groundb, invb, res, dirn, field, part, acc, retb,
    flows, own, outer, inner, mine, total, yhalo, back, listed, landed, mask, list8, list8b, list8row,
    degown, degouter, deginner, degmine, degtotal, degh, dback,
    back_sem, land_sem, deg_sem, line_sem, degline_sem,
):
    first, pairs = chebyshev_terms(ITERS)
    me, z = lax.axis_index("vtx"), lax.axis_index("edg")
    slot, columns = back.shape[2], back.shape[3]
    halo_len = peers * slot
    wide_rows = src_ref.shape[0]
    num_edges = wide_rows * LANES
    num_rows = sol_ref.shape[0]
    high = num_rows // LANES
    ktile = min(1024, num_edges)
    etile = 512
    quarter = num_edges // 4
    groups = num_rows // GROUP
    per = GROUP // PIECE
    count = num_rows // PIECE
    middle = (z + 1) // 2 % 2 == 1
    at_end = (z + 1) // 2 % 2 == 0
    near, far, peer = {"edg": 1 + z // 3}, {"edg": 3 * (z // 2)}, {"edg": 3 - z}
    f32, bf16, i32 = jnp.float32, jnp.bfloat16, jnp.int32

    barrier = pltpu.get_barrier_semaphore()

    def greet(target):
        pl.semaphore_signal(barrier, inc=1, device_id=target, device_id_type=pl.DeviceIdType.MESH)

    def greet_peer(off, _):
        greet({"vtx": lax.rem(me + off, peers)})
        return 0

    lax.fori_loop(1, peers, greet_peer, 0)

    @pl.when(at_end)
    def _():
        greet(near)

    @pl.when(middle)
    def _():
        greet(far)
        greet(peer)

    shape = (wide_rows, LANES)
    position = lax.broadcasted_iota(i32, shape, 0) * LANES + lax.broadcasted_iota(i32, shape, 1)
    live = position < count_ref[0]
    src, dst = src_ref[...], dst_ref[...]
    slots = dst - num_rows
    weight = jnp.where(live, weight_ref[...], 0.0)
    apart = jnp.logical_and(live, src != dst)
    held = jnp.where(apart, weight_ref[...], 0.0)
    root = jnp.sqrt(held)
    mask[...] = jnp.where(apart, 1.0, 0.0)
    peer_of = jnp.where(slots < 0, -1, slots // slot)
    within = jnp.where(slots < 0, -1, slots % slot)
    along = [src, dst, src // LANES, dst // LANES, peer_of]
    for k in range(wide_rows):
        cols = slice(k * LANES, (k + 1) * LANES)
        for row, value in enumerate(along):
            rowf[row : row + 1, cols] = value[k : k + 1, :]
        wide[0:1, cols] = weight[k : k + 1, :]
    src_t, dst_t, within_t = src.T, dst.T, within.T
    held_t, root_t = held.T, root.T
    for k in range(wide_rows):
        rows = slice(k * LANES, (k + 1) * LANES)
        block = (LANES, LANES)
        srow[rows, :] = short(src_t[:, k : k + 1], block)
        dstb[rows, :] = short(dst_t[:, k : k + 1], block)
        wb[rows, :] = jnp.broadcast_to(held_t[:, k : k + 1], block)
    srcb = srow

    lane_e = lax.broadcasted_iota(jnp.int16, (num_edges, LANES), 1)

    def count_up(rows, row, low):
        weights = wide[0:1, :]
        up = lax.broadcasted_iota(i32, (rows, num_edges), 0)
        picked = jnp.where(up == row, weights, 0.0)
        parts = dot(jnp.concatenate(split3(picked), axis=0), low)
        return parts[:rows] + parts[rows : 2 * rows] + parts[2 * rows :]

    for k in range(wide_rows):
        rows = slice(k * LANES, (k + 1) * LANES)
        match = lax.broadcasted_iota(jnp.int16, (LANES, LANES), 1) == short(within_t[:, k : k + 1], (LANES, LANES))
        flows[rows, :LANES] = one_hot(match)
    degree_far = count_up(-(-peers // 16) * 16, rowf[4:5, :], flows[:, :LANES])
    for q in range(peers):
        degh[q] = jnp.broadcast_to(degree_far[q : q + 1, :], (8, LANES))

    pl.semaphore_wait(barrier, peers + jnp.where(middle, 1, 0))

    def degree_of(to):
        return degh.at[to]

    exchange(me, peers, degree_of, dback, deg_sem.at[0], deg_sem.at[1])
    dback[me] = degh[me]

    for k in range(wide_rows):
        rows = slice(k * LANES, (k + 1) * LANES)
        flows[rows, :] = pair(-(root_t[:, k : k + 1] * sketch_ref[rows, :].astype(f32)))

    list8[...] = jnp.full(list8.shape, -1, i32)
    list8[:peers, :slot] = list_ref[...]
    list_t = list8[...].T
    for q in range(peers):
        spread = jnp.broadcast_to(list_t[:, q : q + 1], (LANES, LANES))
        list8b[q * LANES : (q + 1) * LANES, :] = spread.astype(jnp.int16)
        list8row[0:1, q * LANES : (q + 1) * LANES] = list8[q : q + 1, :]
        listb[q * slot : (q + 1) * slot, :] = spread[:slot]
    for at in range(0, halo_len, LANES):
        listrow[0:1, at : at + LANES] = listb[at : at + LANES, :].T[0:1, :]

    ground_t = ground_ref[...].T
    for j in range(high):
        rows = slice(j * LANES, (j + 1) * LANES)
        groundb[rows, :] = jnp.broadcast_to(ground_t[:, j : j + 1], (LANES, LANES))
    for ref in (res, dirn, sol_ref, part):
        ref[...] = jnp.zeros(ref.shape, f32)

    def scatter_rows(at, rows):
        acc[:rows, :] = jnp.zeros((rows, 2 * columns), f32)

        def body(k, _):
            cols = pl.ds(pl.multiple_of(k * ktile, ktile), ktile)
            pick = signed(down_rows(rowf[0:1, cols], at, rows), down_rows(rowf[1:2, cols], at, rows))
            acc[:rows, :] += dot(pick, flows[cols, :])
            return 0

        lax.fori_loop(0, num_edges // ktile, body, 0)
        return halves(acc[:rows, :])

    def edge_hots(rows, at, width):
        hots = zip(along_lanes(srcb[rows, :], at, width), along_lanes(dstb[rows, :], at, width))
        return jnp.concatenate([signed(a, b) for a, b in hots], axis=1)

    def gather_near(group, q):
        for off in range(0, quarter, etile):
            rows = pl.ds(pl.multiple_of(q * quarter + off, etile), etile)
            base = pl.multiple_of(group * GROUP, GROUP)
            hots = edge_hots(rows, base, GROUP)
            part[rows, :] += halves(dot(hots, field[pl.ds(base, GROUP), :]))

    def own_degree():
        low = one_hot(jnp.bitwise_and(srcb[...], jnp.int16(LANES - 1)) == lane_e)
        rows = -(-high // 16) * 16
        got = count_up(rows, rowf[2:3, :], low)
        low = one_hot(jnp.bitwise_and(dstb[...], jnp.int16(LANES - 1)) == lane_e)
        got += count_up(rows, rowf[3:4, :], low)
        up = lax.broadcasted_iota(i32, (rows, peers * LANES), 0)
        for q in range(peers):
            wide[0:1, q * LANES : (q + 1) * LANES] = dback[q, 0:1, :]
        picked = jnp.where(up == list8row[...] // LANES, wide[0:1, : peers * LANES], 0.0)
        lane = lax.broadcasted_iota(jnp.int16, (peers * LANES, LANES), 1)
        low = one_hot(jnp.bitwise_and(list8b[...], jnp.int16(LANES - 1)) == lane)
        parts = dot(jnp.concatenate(split3(picked), axis=0), low)
        got += parts[:rows] + parts[rows : 2 * rows] + parts[2 * rows :]
        degown[...] = got[:high]

    def degree_copy(kind, src, dst, target):
        return remote(src, dst, degline_sem.at[0, kind], degline_sem.at[1, kind], target)

    hpiece = even_piece(halo_len, 512)

    def stage(s, _):
        begin, last = s == 0, s == ITERS - 1
        keep, push = jnp.float32(0.0), jnp.float32(first)
        for at, (k_coef, p_coef) in enumerate(pairs):
            keep = jnp.where(s == at + 1, jnp.float32(k_coef), keep)
            push = jnp.where(s == at + 1, jnp.float32(p_coef), push)

        def line_copy(kind, k, src, dst, target):
            rows = pl.ds(pl.multiple_of(k * PIECE, PIECE), PIECE)
            return remote(
                src.at[s, rows], dst.at[s, rows], line_sem.at[0, s, kind, k], line_sem.at[1, s, kind, k], target
            )

        def to_middle(k):
            return line_copy(0, k, own, outer, near)

        def to_peer(k):
            return line_copy(1, k, mine, inner, peer)

        def to_end(k):
            return line_copy(2, k, total, total, far)

        def from_end(k):
            return line_copy(0, k, own, outer, far)

        def from_middle(k):
            return line_copy(2, k, total, total, near)

        def piece_rows(k):
            return pl.ds(pl.multiple_of(k * PIECE, PIECE), PIECE)

        def pass_partial(k):
            rows = piece_rows(k)
            from_end(k).wait_recv()
            mine[s, rows, :] = own[s, rows, :] + outer[s, rows, :]
            to_peer(k).start()

        def pass_total(k):
            rows = piece_rows(k)
            to_peer(k).wait_recv()
            total[s, rows, :] = mine[s, rows, :] + inner[s, rows, :]
            to_end(k).start()

        for at in range(0, halo_len, hpiece):
            yhalo[s, at : at + hpiece, :] = scatter_rows(num_rows + at, hpiece)

        def halo_of(to):
            return yhalo.at[s, pl.ds(pl.multiple_of(to * slot, 8), slot)]

        back_args = (me, peers, halo_of, back.at[s], back_sem.at[0, s], back_sem.at[1, s])
        exchange(*back_args)
        back[s, me] = yhalo[s, pl.ds(pl.multiple_of(me * slot, 8), slot), :]

        def group_rows(c, _):
            at = pl.multiple_of(c * GROUP, GROUP)
            local = scatter_rows(at, GROUP)

            @pl.when(jnp.logical_and(begin, c == 0))
            def _():
                exchange_wait(me, peers, degree_of, dback, deg_sem.at[0], deg_sem.at[1])
                own_degree()

            @pl.when(c == 0)
            def _():
                exchange_wait(*back_args)
                retb[...] = pair(back[s].reshape(halo_len, columns))

            @pl.when(jnp.logical_and(begin, c == 0))
            def _():
                @pl.when(at_end)
                def _():
                    degree_copy(0, degown, degouter, near).start()

            pick = one_hot(down_rows(listrow[...], at, GROUP))
            own[s, pl.ds(at, GROUP), :] = local + halves(dot(pick, retb[...]))

            @pl.when(at_end)
            def _():
                for j in range(per):
                    to_middle(c * per + j).start()

            @pl.when(jnp.logical_and(middle, c == groups - 2))
            def _():
                @pl.when(begin)
                def _():
                    degree_copy(0, degown, degouter, far).wait_recv()
                    degmine[...] = degown[...] + degouter[...]
                    degree_copy(1, degmine, deginner, peer).start()

                for k in range(LAG):
                    pass_partial(k)

            return 0

        lax.fori_loop(0, groups, group_rows, 0)

        @pl.when(begin)
        def _():
            @pl.when(middle)
            def _():
                degree_copy(1, degmine, deginner, peer).wait_recv()
                degtotal[...] = degmine[...] + deginner[...]
                degree_copy(2, degtotal, degtotal, far).start()

            @pl.when(at_end)
            def _():
                degree_copy(2, degtotal, degtotal, near).wait_recv()

            inverse_t = (1.0 / (degtotal[...] + ground_ref[...])).T
            for j in range(high):
                rows = slice(j * LANES, (j + 1) * LANES)
                invb[rows, :] = jnp.broadcast_to(inverse_t[:, j : j + 1], (LANES, LANES))

        def step(k, _):
            rows = piece_rows(k)

            @pl.when(middle)
            def _():
                @pl.when(k + LAG < count)
                def _():
                    pass_partial(k + LAG)

                pass_total(k)

            @pl.when(at_end)
            def _():
                from_middle(k).wait_recv()

            old = dirn[rows, :]
            residual = res[rows, :] - (groundb[rows, :] * old + total[s, rows, :])
            direction = keep * old + push * invb[rows, :] * residual
            shown = sol_ref[rows, :] + direction
            res[rows, :] = residual
            dirn[rows, :] = direction
            sol_ref[rows, :] = shown
            field[rows, :] = pair(jnp.where(last, shown, direction))
            group, j = k // per, lax.rem(k, per)

            @pl.when(j == per - 1)
            def _():
                base = pl.multiple_of(group * GROUP, GROUP)
                for at in range(0, halo_len, hpiece):
                    spread = listb[at : at + hpiece, :].astype(jnp.int16)
                    hots = jnp.concatenate([one_hot(m) for m in along_lanes(spread, base, GROUP)], axis=1)
                    got = halves(dot(hots, field[pl.ds(base, GROUP), :]))
                    listed[s, at : at + hpiece, :] = jnp.where(group == 0, got, listed[s, at : at + hpiece, :] + got)

            @pl.when(group > 0)
            def _():
                gather_near(group - 1, j)

            return 0

        lax.fori_loop(0, count, step, 0)

        def listed_of(to):
            return listed.at[s, pl.ds(pl.multiple_of(to * slot, 8), slot)]

        land_args = (me, peers, listed_of, landed.at[s], land_sem.at[0, s], land_sem.at[1, s])
        exchange(*land_args)
        landed[s, me] = listed[s, pl.ds(pl.multiple_of(me * slot, 8), slot), :]

        def near_tail(q, _):
            gather_near(groups - 1, q)
            return 0

        lax.fori_loop(0, 4, near_tail, 0)
        exchange_wait(*land_args)
        field[num_rows:, :] = pair(landed[s].reshape(halo_len, columns))

        def gather_far(k):
            rows = pl.ds(pl.multiple_of(k * etile, etile), etile)
            gap = part[rows, :] + halves(dot(edge_hots(rows, num_rows, halo_len), field[num_rows:, :]))
            part[rows, :] = jnp.zeros(gap.shape, f32)
            return rows, gap

        @pl.when(jnp.logical_not(last))
        def _():
            def make_flows(k, _):
                rows, gap = gather_far(k)
                flows[rows, :] = pair(gap * wb[rows, :])
                return 0

            lax.fori_loop(0, num_edges // etile, make_flows, 0)

        @pl.when(last)
        def _():
            def make_gaps(k, _):
                rows, gap = gather_far(k)
                square = gap * gap
                for i in range(etile // LANES):
                    block = square[i * LANES : (i + 1) * LANES, :].T
                    row = pl.ds(k * (etile // LANES) + i, 1)
                    gap_ref[row, :] = mask[row, :] * jnp.sum(block, axis=0, keepdims=True) / columns
                return 0

            lax.fori_loop(0, num_edges // etile, make_gaps, 0)

        def line_done(k, _):
            @pl.when(at_end)
            def _():
                to_middle(k).wait_send()

            @pl.when(middle)
            def _():
                to_peer(k).wait_send()
                to_end(k).wait_send()

            return 0

        lax.fori_loop(0, count, line_done, 0)
        return 0

    lax.fori_loop(0, ITERS, stage, 0)

    @pl.when(at_end)
    def _():
        degree_copy(0, degown, degouter, near).wait_send()

    @pl.when(middle)
    def _():
        degree_copy(1, degmine, deginner, peer).wait_send()
        degree_copy(2, degtotal, degtotal, far).wait_send()


def local(sketch_cols, edge_weight, ground, src_local, dst_index, send_rows, edge_count):
    peers = lax.axis_size("vtx")
    num_rows, num_edges = ground.shape[0], edge_weight.shape[0]
    slot, columns = send_rows.shape[2], sketch_cols.shape[1]
    halo_len, high, wide_rows = peers * slot, num_rows // LANES, num_edges // LANES
    count = num_rows // PIECE
    f32, bf16, i32, i16 = jnp.float32, jnp.bfloat16, jnp.int32, jnp.int16
    vmem, dma = pltpu.VMEM, pltpu.SemaphoreType.DMA
    peers8 = -(-peers // 8) * 8
    halo = vmem((ITERS, peers, slot, columns), f32)
    flat_halo = vmem((ITERS, halo_len, columns), f32)
    rows_f32 = vmem((num_rows, columns), f32)
    line = vmem((ITERS, num_rows, columns), f32)
    small = vmem((high, LANES), f32)
    spread = vmem((num_edges, LANES), i16)
    scratch = [
        vmem((8, num_edges), i32), spread, spread,
        vmem((8, max(num_edges, peers * LANES)), f32), vmem((num_edges, LANES), f32),
        vmem((halo_len, LANES), i32), vmem((1, halo_len), i32),
        rows_f32, rows_f32, rows_f32, rows_f32,
        vmem((num_rows + halo_len, 2 * columns), bf16), vmem((num_edges, columns), f32),
        vmem((GROUP, 2 * columns), f32), vmem((halo_len, 2 * columns), bf16),
        vmem((num_edges, 2 * columns), bf16), line, line, line, line, line,
        flat_halo, halo, flat_halo, halo,
        vmem((wide_rows, LANES), f32), vmem((peers8, LANES), i32),
        vmem((peers * LANES, LANES), i16), vmem((1, peers * LANES), i32),
        small, small, small, small, small, vmem((peers, 8, LANES), f32), vmem((peers, 8, LANES), f32),
        dma((2, ITERS, peers)), dma((2, ITERS, peers)), dma((2, peers)), dma((2, ITERS, 3, count)), dma((2, 3)),
    ]
    in_vmem = pl.BlockSpec(memory_space=pltpu.VMEM)
    solution, gaps = pl.pallas_call(
        functools.partial(kernel, peers),
        in_specs=[in_vmem] * 6 + [pl.BlockSpec(memory_space=pltpu.SMEM)],
        out_specs=[in_vmem] * 2,
        out_shape=[jax.ShapeDtypeStruct((num_rows, columns), f32), jax.ShapeDtypeStruct((wide_rows, LANES), f32)],
        scratch_shapes=scratch,
        compiler_params=pltpu.CompilerParams(collective_id=0, has_side_effects=True, vmem_limit_bytes=VMEM_LIMIT),
        name="sketch",
    )(
        sketch_cols, edge_weight.reshape(wide_rows, LANES), ground.reshape(high, LANES),
        src_local.reshape(wide_rows, LANES), dst_index.reshape(wide_rows, LANES), send_rows[0], edge_count,
    )
    return solution, gaps.reshape(-1)


def solution(mesh):
    in_specs = (
        P(("vtx", "edg"), None),
        P(("vtx", "edg")),
        P("vtx"),
        P(("vtx", "edg")),
        P(("vtx", "edg")),
        P(("vtx", "edg"), None, None),
        P(("vtx", "edg")),
    )
    out_specs = (P("vtx", None), P(("vtx", "edg")))
    return jax.shard_map(local, mesh=mesh, in_specs=in_specs, out_specs=out_specs, check_vma=False)
```

```python
import functools

import jax
import jax.numpy as jnp
from jax import lax
from jax.experimental import pallas as pl
from jax.experimental.pallas import tpu as pltpu
from jax.sharding import PartitionSpec as P

ITERS = 3

lam_low = 0.05
lam_high = 2.0
LANES = 128
VMEM_LIMIT = 62 * 1024 * 1024
GROUP = 512
PIECE = 128
LAG = 3


def chebyshev_terms(steps):
    centre = (lam_high + lam_low) / 2.0
    half_width = (lam_high - lam_low) / 2.0
    sigma_val = centre / half_width
    rho_prev = 1.0 / sigma_val
    pairs = []
    for count_idx in range(steps - 1):
        rho_next = 1.0 / (2.0 * sigma_val - rho_prev)
        pairs.append((rho_next * rho_prev, 2.0 * rho_next / half_width))
        rho_prev = rho_next
    return (1.0 / centre, pairs)


def split2(x):
    hi = x.astype(jnp.bfloat16)
    lo = (x - hi.astype(jnp.float32)).astype(jnp.bfloat16)
    return hi, lo


def split3(x):
    hi = x.astype(jnp.bfloat16)
    rest = x - hi.astype(jnp.float32)
    mid, lo = split2(rest)
    return hi, mid, lo


def pair(x):
    return jnp.concatenate(split2(x), axis=1)


def halves(x):
    n = x.shape[1] // 2
    return x[:, :n] + x[:, n:]


def dot(a, b):
    return jnp.dot(a, b, preferred_element_type=jnp.float32)


def dot_lanes(a, b):
    return lax.dot_general(a, b, (((1,), (1,)), ((), ())), preferred_element_type=jnp.float32)


def signed(is_src, is_dst):
    one, none = jnp.ones(is_src.shape, jnp.bfloat16), jnp.zeros(is_src.shape, jnp.bfloat16)
    return jnp.where(is_src, one, jnp.where(is_dst, -one, none))


def one_hot(match):
    return jnp.where(match, jnp.ones(match.shape, jnp.bfloat16), jnp.zeros(match.shape, jnp.bfloat16))


def short(x, shape):
    return jnp.broadcast_to(jnp.asarray(x, jnp.int32), shape).astype(jnp.int16)


def down_rows(row, at, rows):
    shape = (rows, row.shape[1])
    return lax.broadcasted_iota(jnp.int16, shape, 0) == jnp.broadcast_to((row - at).astype(jnp.int16), shape)


def along_lanes(spread, at, width):
    parts = []
    lane = lax.broadcasted_iota(jnp.int16, spread.shape, 1)
    for off in range(0, width, LANES):
        parts.append(lane + short(at + off, spread.shape) == spread)
    return parts


def even_piece(total, most):
    return max(n for n in range(8, most + 1, 8) if total % n == 0)


def remote(src, dst, send_sem, recv_sem, target):
    return pltpu.make_async_remote_copy(
        src_ref=src, dst_ref=dst, send_sem=send_sem, recv_sem=recv_sem,
        device_id=target, device_id_type=pl.DeviceIdType.MESH,
    )


def exchange(me, peers, src, dst, send_sem, recv_sem):
    def start(off, _):
        to = lax.rem(me + off, peers)
        remote(src(to), dst.at[me], send_sem.at[off], recv_sem.at[off], {"vtx": to}).start()
        return 0

    lax.fori_loop(1, peers, start, 0)


def exchange_wait(me, peers, src, dst, send_sem, recv_sem):
    def wait(off, _):
        to = lax.rem(me + off, peers)
        origin = lax.rem(me + peers - off, peers)
        remote(src(to), dst.at[origin], send_sem.at[off], recv_sem.at[off], {"vtx": to}).wait()
        return 0

    lax.fori_loop(1, peers, wait, 0)


def kernel(
    peers, sketch_ref, weight_ref, ground_ref, src_ref, dst_ref, list_ref, count_ref, sol_ref, gap_ref,
    rowf, srcb, dstb, wide, wb, listb, listrow, groundb, invb, res, dirn, field, part, acc, retb,
    flows, own, outer, inner, mine, total, yhalo, back, listed, landed, mask, list8, list8row,
    degown, degouter, deginner, degmine, degtotal, degh, dback,
    back_sem, land_sem, deg_sem, line_sem, degline_sem,
):
    first, pairs = chebyshev_terms(ITERS)
    me, z = lax.axis_index("vtx"), lax.axis_index("edg")
    slot, columns = back.shape[2], back.shape[3]
    halo_len = peers * slot
    wide_rows = src_ref.shape[0]
    num_edges = wide_rows * LANES
    num_rows = sol_ref.shape[0]
    high = num_rows // LANES
    ktile = min(1024, num_edges)
    etile = 1024
    quarter = num_edges // 4
    groups = num_rows // GROUP
    per = GROUP // PIECE
    count = num_rows // PIECE
    middle = (z + 1) // 2 % 2 == 1
    at_end = (z + 1) // 2 % 2 == 0
    near, far, peer = {"edg": 1 + z // 3}, {"edg": 3 * (z // 2)}, {"edg": 3 - z}
    f32, bf16, i32 = jnp.float32, jnp.bfloat16, jnp.int32

    barrier = pltpu.get_barrier_semaphore()

    def greet(target):
        pl.semaphore_signal(barrier, inc=1, device_id=target, device_id_type=pl.DeviceIdType.MESH)

    def greet_peer(off, _):
        greet({"vtx": lax.rem(me + off, peers)})
        return 0

    lax.fori_loop(1, peers, greet_peer, 0)

    @pl.when(at_end)
    def _():
        greet(near)

    @pl.when(middle)
    def _():
        greet(far)
        greet(peer)

    shape = (wide_rows, LANES)
    position = lax.broadcasted_iota(i32, shape, 0) * LANES + lax.broadcasted_iota(i32, shape, 1)
    live = position < count_ref[0]
    src, dst = src_ref[...], dst_ref[...]
    slots = dst - num_rows
    weight = jnp.where(live, weight_ref[...], 0.0)
    apart = jnp.logical_and(live, src != dst)
    held = jnp.where(apart, weight_ref[...], 0.0)
    root = jnp.sqrt(held)
    mask[...] = jnp.where(apart, 1.0, 0.0)
    peer_of = jnp.where(slots < 0, -1, slots // slot)
    within = jnp.where(slots < 0, -1, slots % slot)
    for k in range(wide_rows):
        cols = slice(k * LANES, (k + 1) * LANES)
        rowf[0:1, cols] = src[k : k + 1, :]
        rowf[1:2, cols] = dst[k : k + 1, :]
        rowf[2:3, cols] = peer_of[k : k + 1, :]
        rowf[3:4, cols] = within[k : k + 1, :]
        wide[0:1, cols] = weight[k : k + 1, :]

    root_t = root.T
    for k in range(wide_rows):
        rows = slice(k * LANES, (k + 1) * LANES)
        flows[rows, :] = pair(-(root_t[:, k : k + 1] * sketch_ref[rows, :].astype(f32)))

    def spread_columns():
        for values, store in ((src_ref[...], srcb), (dst_ref[...], dstb), (held, wb)):
            turned = values.T
            for k in range(wide_rows):
                rows = slice(k * LANES, (k + 1) * LANES)
                store[rows, :] = jnp.broadcast_to(turned[:, k : k + 1], (LANES, LANES)).astype(store.dtype)
        for ref in (res, dirn, sol_ref, part):
            ref[...] = jnp.zeros(ref.shape, f32)

    def count_up(rows, up_at, low, weights):
        edges = weights.shape[1]
        up = lax.broadcasted_iota(i32, (rows, edges), 0)
        picked = jnp.where(up == up_at, weights, 0.0)
        parts = dot_lanes(jnp.concatenate(split3(picked), axis=0), one_hot(down_rows(low, 0, LANES)))
        return parts[:rows] + parts[rows : 2 * rows] + parts[2 * rows :]

    def degree_of(to):
        return degh.at[to]

    def far_degree():
        got = count_up(-(-peers // 16) * 16, rowf[2:3, :], rowf[3:4, :], wide[0:1, :num_edges])
        for q in range(peers):
            degh[q] = jnp.broadcast_to(got[q : q + 1, :], (8, LANES))
        exchange(me, peers, degree_of, dback, deg_sem.at[0], deg_sem.at[1])
        dback[me] = degh[me]

    def spread_lists():
        list8[...] = jnp.full(list8.shape, -1, i32)
        list8[:peers, :slot] = list_ref[...]
        list_t = list8[...].T
        for q in range(peers):
            list8row[0:1, q * LANES : (q + 1) * LANES] = list8[q : q + 1, :]
            listb[q * slot : (q + 1) * slot, :] = jnp.broadcast_to(list_t[:, q : q + 1], (LANES, LANES))[:slot]
        for at in range(0, halo_len, LANES):
            listrow[0:1, at : at + LANES] = listb[at : at + LANES, :].T[0:1, :]

    def scatter_rows(at, rows):
        acc[:rows, :] = jnp.zeros((rows, 2 * columns), f32)

        def body(k, _):
            cols = pl.ds(pl.multiple_of(k * ktile, ktile), ktile)
            pick = signed(down_rows(rowf[0:1, cols], at, rows), down_rows(rowf[1:2, cols], at, rows))
            acc[:rows, :] += dot(pick, flows[cols, :])
            return 0

        lax.fori_loop(0, num_edges // ktile, body, 0)
        return halves(acc[:rows, :])

    def edge_hots(rows, at, width):
        hots = zip(along_lanes(srcb[rows, :], at, width), along_lanes(dstb[rows, :], at, width))
        return jnp.concatenate([signed(a, b) for a, b in hots], axis=1)

    def gather_near(group, q, tail=False):
        for off in range(0, quarter, etile):
            rows = pl.ds(pl.multiple_of(q * quarter + off, etile), etile)
            base = pl.multiple_of(group * GROUP, GROUP)
            hots = edge_hots(rows, base, GROUP)
            got = part[rows, :] + halves(dot(hots, field[pl.ds(base, GROUP), :]))
            part[rows, :] = got
            if tail:
                flows[rows, :] = pair(got * wb[rows, :])

    def own_degree():
        rows = -(-high // 16) * 16
        got = jnp.zeros((rows, LANES), f32)
        for row in (0, 1):
            at = rowf[row : row + 1, :]
            got += count_up(rows, at // LANES, at % LANES, wide[0:1, :num_edges])
        for q in range(peers):
            wide[1:2, q * LANES : (q + 1) * LANES] = dback[q, 0:1, :]
        at = list8row[...]
        landing = count_up(rows, jnp.where(at < 0, -1, at // LANES), at % LANES, wide[1:2, : peers * LANES])
        degown[:high, :] = (got + landing)[:high]
        degown[high:, :] = landing[:high]

    def degree_copy(kind, src, dst, target):
        return remote(src, dst, degline_sem.at[0, kind], degline_sem.at[1, kind], target)

    hpiece = even_piece(halo_len, 512)

    def back_of(s):
        def halo_of(to):
            return yhalo.at[s, pl.ds(pl.multiple_of(to * slot, 8), slot)]

        return me, peers, halo_of, back.at[s], back_sem.at[0, s], back_sem.at[1, s]

    def send_back(s):
        for at in range(0, halo_len, hpiece):
            yhalo[s, at : at + hpiece, :] = scatter_rows(num_rows + at, hpiece)

        if isinstance(s, int):
            pl.semaphore_wait(barrier, peers + jnp.where(middle, 1, 0))
        exchange(*back_of(s))
        back[s, me] = yhalo[s, pl.ds(pl.multiple_of(me * slot, 8), slot), :]

    send_back(0)
    far_degree()
    spread_lists()

    def stage(s, _):
        begin, last = s == 0, s == ITERS - 1
        keep, push = jnp.float32(0.0), jnp.float32(first)
        for at, (k_coef, p_coef) in enumerate(pairs):
            keep = jnp.where(s == at + 1, jnp.float32(k_coef), keep)
            push = jnp.where(s == at + 1, jnp.float32(p_coef), push)

        def line_copy(kind, k, src, dst, target):
            rows = pl.ds(pl.multiple_of(k * PIECE, PIECE), PIECE)
            return remote(
                src.at[s, rows], dst.at[s, rows], line_sem.at[0, s, kind, k], line_sem.at[1, s, kind, k], target
            )

        def to_middle(k):
            return line_copy(0, k, own, outer, near)

        def to_peer(k):
            return line_copy(1, k, mine, inner, peer)

        def to_end(k):
            return line_copy(2, k, total, total, far)

        def from_end(k):
            return line_copy(0, k, own, outer, far)

        def from_middle(k):
            return line_copy(2, k, total, total, near)

        def piece_rows(k):
            return pl.ds(pl.multiple_of(k * PIECE, PIECE), PIECE)

        def pass_partial(k):
            rows = piece_rows(k)
            from_end(k).wait_recv()
            mine[s, rows, :] = own[s, rows, :] + outer[s, rows, :]
            to_peer(k).start()

        def pass_total(k):
            rows = piece_rows(k)
            to_peer(k).wait_recv()
            total[s, rows, :] = mine[s, rows, :] + inner[s, rows, :]
            to_end(k).start()

        back_args = back_of(s)

        def group_rows(c, _):
            at = pl.multiple_of(c * GROUP, GROUP)
            local = scatter_rows(at, GROUP)

            @pl.when(c == 0)
            def _():
                exchange_wait(*back_args)
                retb[...] = pair(back[s].reshape(halo_len, columns))

            pick = one_hot(down_rows(listrow[...], at, GROUP))
            own[s, pl.ds(at, GROUP), :] = local + halves(dot(pick, retb[...]))

            @pl.when(at_end)
            def _():
                for j in range(per):
                    to_middle(c * per + j).start()

            @pl.when(jnp.logical_and(begin, c == 0))
            def _():
                exchange_wait(me, peers, degree_of, dback, deg_sem.at[0], deg_sem.at[1])
                own_degree()

                @pl.when(at_end)
                def _():
                    degree_copy(0, degown, degouter, near).start()

                spread_columns()

            @pl.when(jnp.logical_and(middle, c == groups - 2))
            def _():
                @pl.when(begin)
                def _():
                    degree_copy(0, degown, degouter, far).wait_recv()
                    degmine[...] = degown[...] + degouter[...]
                    degree_copy(1, degmine, deginner, peer).start()

                for k in range(LAG):
                    pass_partial(k)

            return 0

        lax.fori_loop(0, groups, group_rows, 0)

        @pl.when(begin)
        def _():
            @pl.when(middle)
            def _():
                degree_copy(1, degmine, deginner, peer).wait_recv()
                degtotal[...] = degmine[...] + deginner[...]
                degree_copy(2, degtotal, degtotal, far).start()

            @pl.when(at_end)
            def _():
                degree_copy(2, degtotal, degtotal, near).wait_recv()

            inverse_t = (1.0 / (degtotal[:high, :] + ground_ref[...])).T
            held_t = (degtotal[high:, :] + ground_ref[...]).T
            for j in range(high):
                rows = slice(j * LANES, (j + 1) * LANES)
                invb[rows, :] = jnp.broadcast_to(inverse_t[:, j : j + 1], (LANES, LANES))
                groundb[rows, :] = jnp.broadcast_to(held_t[:, j : j + 1], (LANES, LANES))

        def step(k, _):
            rows = piece_rows(k)

            @pl.when(middle)
            def _():
                @pl.when(k + LAG < count)
                def _():
                    pass_partial(k + LAG)

                pass_total(k)

            @pl.when(at_end)
            def _():
                from_middle(k).wait_recv()

            old = dirn[rows, :]
            residual = res[rows, :] - (groundb[rows, :] * old + total[s, rows, :])
            direction = keep * old + push * invb[rows, :] * residual
            shown = sol_ref[rows, :] + direction
            res[rows, :] = residual
            dirn[rows, :] = direction
            sol_ref[rows, :] = shown
            field[rows, :] = pair(jnp.where(last, shown, direction))
            group, j = k // per, lax.rem(k, per)

            @pl.when(j == per - 1)
            def _():
                base = pl.multiple_of(group * GROUP, GROUP)
                for at in range(0, halo_len, hpiece):
                    spread = listb[at : at + hpiece, :].astype(jnp.int16)
                    hots = jnp.concatenate([one_hot(m) for m in along_lanes(spread, base, GROUP)], axis=1)
                    got = halves(dot(hots, field[pl.ds(base, GROUP), :]))
                    listed[s, at : at + hpiece, :] = jnp.where(group == 0, got, listed[s, at : at + hpiece, :] + got)

            @pl.when(group > 0)
            def _():
                gather_near(group - 1, j)

            return 0

        lax.fori_loop(0, count, step, 0)

        def listed_of(to):
            return listed.at[s, pl.ds(pl.multiple_of(to * slot, 8), slot)]

        land_args = (me, peers, listed_of, landed.at[s], land_sem.at[0, s], land_sem.at[1, s])
        exchange(*land_args)
        landed[s, me] = listed[s, pl.ds(pl.multiple_of(me * slot, 8), slot), :]

        def near_tail(q, _):
            gather_near(groups - 1, q, True)
            return 0

        lax.fori_loop(0, 4, near_tail, 0)

        @pl.when(jnp.logical_not(last))
        def _():
            send_back(s + 1)

        exchange_wait(*land_args)
        field[num_rows:, :] = pair(landed[s].reshape(halo_len, columns))

        def gather_far(k):
            rows = pl.ds(pl.multiple_of(k * etile, etile), etile)
            gap = part[rows, :] + halves(dot(edge_hots(rows, num_rows, halo_len), field[num_rows:, :]))
            part[rows, :] = jnp.zeros(gap.shape, f32)
            return rows, gap

        @pl.when(jnp.logical_not(last))
        def _():
            def make_flows(k, _):
                rows, gap = gather_far(k)
                flows[rows, :] = pair(gap * wb[rows, :])
                return 0

            lax.fori_loop(0, num_edges // etile, make_flows, 0)

        @pl.when(last)
        def _():
            def make_gaps(k, _):
                rows, gap = gather_far(k)
                square = gap * gap
                for i in range(etile // LANES):
                    block = square[i * LANES : (i + 1) * LANES, :].T
                    row = pl.ds(k * (etile // LANES) + i, 1)
                    gap_ref[row, :] = mask[row, :] * jnp.sum(block, axis=0, keepdims=True) / columns
                return 0

            lax.fori_loop(0, num_edges // etile, make_gaps, 0)

        def line_done(k, _):
            @pl.when(at_end)
            def _():
                to_middle(k).wait_send()

            @pl.when(middle)
            def _():
                to_peer(k).wait_send()
                to_end(k).wait_send()

            return 0

        lax.fori_loop(0, count, line_done, 0)
        return 0

    lax.fori_loop(0, ITERS, stage, 0)

    @pl.when(at_end)
    def _():
        degree_copy(0, degown, degouter, near).wait_send()

    @pl.when(middle)
    def _():
        degree_copy(1, degmine, deginner, peer).wait_send()
        degree_copy(2, degtotal, degtotal, far).wait_send()


def local(sketch_cols, edge_weight, ground, src_local, dst_index, send_rows, edge_count):
    peers = lax.axis_size("vtx")
    num_rows, num_edges = ground.shape[0], edge_weight.shape[0]
    slot, columns = send_rows.shape[2], sketch_cols.shape[1]
    halo_len, high, wide_rows = peers * slot, num_rows // LANES, num_edges // LANES
    count = num_rows // PIECE
    f32, bf16, i32, i16 = jnp.float32, jnp.bfloat16, jnp.int32, jnp.int16
    vmem, dma = pltpu.VMEM, pltpu.SemaphoreType.DMA
    peers8 = -(-peers // 8) * 8
    halo = vmem((ITERS, peers, slot, columns), f32)
    flat_halo = vmem((ITERS, halo_len, columns), f32)
    rows_f32 = vmem((num_rows, columns), f32)
    line = vmem((ITERS, num_rows, columns), f32)
    small = vmem((2 * high, LANES), f32)
    spread = vmem((num_edges, LANES), i16)
    scratch = [
        vmem((8, num_edges), i32), spread, spread,
        vmem((8, max(num_edges, peers * LANES)), f32), vmem((num_edges, LANES), f32),
        vmem((halo_len, LANES), i32), vmem((1, halo_len), i32),
        rows_f32, rows_f32, rows_f32, rows_f32,
        vmem((num_rows + halo_len, 2 * columns), bf16), vmem((num_edges, columns), f32),
        vmem((GROUP, 2 * columns), f32), vmem((halo_len, 2 * columns), bf16),
        vmem((num_edges, 2 * columns), bf16), line, line, line, line, line,
        flat_halo, halo, flat_halo, halo,
        vmem((wide_rows, LANES), f32), vmem((peers8, LANES), i32),
        vmem((1, peers * LANES), i32),
        small, small, small, small, small, vmem((peers, 8, LANES), f32), vmem((peers, 8, LANES), f32),
        dma((2, ITERS, peers)), dma((2, ITERS, peers)), dma((2, peers)), dma((2, ITERS, 3, count)), dma((2, 3)),
    ]
    in_vmem = pl.BlockSpec(memory_space=pltpu.VMEM)
    solution, gaps = pl.pallas_call(
        functools.partial(kernel, peers),
        in_specs=[in_vmem] * 6 + [pl.BlockSpec(memory_space=pltpu.SMEM)],
        out_specs=[in_vmem] * 2,
        out_shape=[jax.ShapeDtypeStruct((num_rows, columns), f32), jax.ShapeDtypeStruct((wide_rows, LANES), f32)],
        scratch_shapes=scratch,
        compiler_params=pltpu.CompilerParams(collective_id=0, has_side_effects=True, vmem_limit_bytes=VMEM_LIMIT),
        name="sketch",
    )(
        sketch_cols, edge_weight.reshape(wide_rows, LANES), ground.reshape(high, LANES),
        src_local.reshape(wide_rows, LANES), dst_index.reshape(wide_rows, LANES), send_rows[0], edge_count,
    )
    return solution, gaps.reshape(-1)


def solution(mesh):
    in_specs = (
        P(("vtx", "edg"), None),
        P(("vtx", "edg")),
        P("vtx"),
        P(("vtx", "edg")),
        P(("vtx", "edg")),
        P(("vtx", "edg"), None, None),
        P(("vtx", "edg")),
    )
    out_specs = (P("vtx", None), P(("vtx", "edg")))
    return jax.shard_map(local, mesh=mesh, in_specs=in_specs, out_specs=out_specs, check_vma=False)
```

```python
import functools

import jax
import jax.numpy as jnp
from jax import lax
from jax.experimental import pallas as pl
from jax.experimental.pallas import tpu as pltpu
from jax.sharding import PartitionSpec as P

ITERS = 3

lam_low = 0.05
lam_high = 2.0
LANES = 128
VMEM_LIMIT = 62 * 1024 * 1024
GROUP = 512
PIECE = 128
LAG = 4
LEAD = 2


def chebyshev_terms(steps):
    centre = (lam_high + lam_low) / 2.0
    half_width = (lam_high - lam_low) / 2.0
    sigma_val = centre / half_width
    rho_prev = 1.0 / sigma_val
    pairs = []
    for count_idx in range(steps - 1):
        rho_next = 1.0 / (2.0 * sigma_val - rho_prev)
        pairs.append((rho_next * rho_prev, 2.0 * rho_next / half_width))
        rho_prev = rho_next
    return (1.0 / centre, pairs)


def split2(x):
    hi = x.astype(jnp.bfloat16)
    lo = (x - hi.astype(jnp.float32)).astype(jnp.bfloat16)
    return hi, lo


def split3(x):
    hi = x.astype(jnp.bfloat16)
    rest = x - hi.astype(jnp.float32)
    mid, lo = split2(rest)
    return hi, mid, lo


def pair(x):
    return jnp.concatenate(split2(x), axis=1)


def halves(x):
    n = x.shape[1] // 2
    return x[:, :n] + x[:, n:]


def dot(a, b):
    return jnp.dot(a, b, preferred_element_type=jnp.float32)


def dot_lanes(a, b):
    return lax.dot_general(a, b, (((1,), (1,)), ((), ())), preferred_element_type=jnp.float32)


def signed(is_src, is_dst):
    one, none = jnp.ones(is_src.shape, jnp.bfloat16), jnp.zeros(is_src.shape, jnp.bfloat16)
    return jnp.where(is_src, one, jnp.where(is_dst, -one, none))


def one_hot(match):
    return jnp.where(match, jnp.ones(match.shape, jnp.bfloat16), jnp.zeros(match.shape, jnp.bfloat16))


def short(x, shape):
    return jnp.broadcast_to(jnp.asarray(x, jnp.int32), shape).astype(jnp.int16)


def down_rows(row, at, rows):
    shape = (rows, row.shape[1])
    return lax.broadcasted_iota(jnp.int16, shape, 0) == jnp.broadcast_to((row - at).astype(jnp.int16), shape)


def along_lanes(spread, at, width):
    parts = []
    lane = lax.broadcasted_iota(jnp.int16, spread.shape, 1)
    for off in range(0, width, LANES):
        parts.append(lane + short(at + off, spread.shape) == spread)
    return parts


def even_piece(total, most):
    return max(n for n in range(8, most + 1, 8) if total % n == 0)


def remote(src, dst, send_sem, recv_sem, target):
    return pltpu.make_async_remote_copy(
        src_ref=src, dst_ref=dst, send_sem=send_sem, recv_sem=recv_sem,
        device_id=target, device_id_type=pl.DeviceIdType.MESH,
    )


def exchange(place, src, dst, send_sem, recv_sem):
    me, peers, target = place

    def start(off, _):
        to = lax.rem(me + off, peers)
        remote(src(to), dst.at[me], send_sem.at[off], recv_sem.at[off], target(to)).start()
        return 0

    lax.fori_loop(1, peers, start, 0)


def exchange_wait(place, src, dst, send_sem, recv_sem):
    me, peers, target = place

    def wait(off, _):
        to = lax.rem(me + off, peers)
        origin = lax.rem(me + peers - off, peers)
        remote(src(to), dst.at[origin], send_sem.at[off], recv_sem.at[off], target(to)).wait()
        return 0

    lax.fori_loop(1, peers, wait, 0)


def kernel(
    peers, sketch_ref, weight_ref, ground_ref, src_ref, dst_ref, list_ref, count_ref, out_ref, gap_ref,
    rowf, srcb, dstb, wide, wb, listb, listrow, groundb, invb, res, dirn, sol, field, part, acc, retb,
    flows, own, outer, inner, mine, total, yhalo, back, listed, landed, mask, list8, list8row,
    degown, degouter, deginner, degmine, degtotal, degh, dback,
    new_src, new_dst, held, new_held, new_list, new_ground, gaps, gaps_in, sol_in,
    back_sem, land_sem, deg_sem, line_sem, degline_sem, swap_sem, sol_sem,
):
    first, pairs = chebyshev_terms(ITERS)
    me, z = lax.axis_index("vtx"), lax.axis_index("edg")
    slot, columns = back.shape[2], back.shape[3]
    halo_len = peers * slot
    wide_rows = src_ref.shape[0]
    num_edges = wide_rows * LANES
    num_rows = out_ref.shape[0]
    high = num_rows // LANES
    ktile = min(1024, num_edges)
    etile = 1024
    quarter = num_edges // 4
    groups = num_rows // GROUP
    per = GROUP // PIECE
    count = num_rows // PIECE
    core, half = lax.rem(me, 2), z // 2

    def mirrored(at):
        return at + core * (3 - 2 * at)

    u = mirrored(z)
    moves = u >= 2
    stays = u < 2
    block = 2 * (me // 2) + half
    other_core = {"vtx": me + 1 - 2 * core}
    across = {"edg": z + 1 - 2 * lax.rem(z, 2)}
    swap_with = {"vtx": me + 1 - 2 * core, "edg": z + 2 - 4 * half}
    inward = {"edg": mirrored(jnp.where(u == 0, 1, u - 1))}
    totals_to = [other_core, {"edg": mirrored(0)}, {"vtx": me + 1 - 2 * core, "edg": mirrored(0)}]
    outward = {"edg": mirrored(jnp.where(u == 1, 2, 3))}

    def home(to):
        return {"vtx": to}

    def hosted(to):
        return {"vtx": 2 * (to // 2) + core, "edg": 2 * lax.rem(to, 2) + lax.rem(z, 2)}

    at_home, at_host = (me, peers, home), (block, peers, hosted)
    f32, bf16, i32 = jnp.float32, jnp.bfloat16, jnp.int32

    barrier = pltpu.get_barrier_semaphore()

    def greet(target):
        pl.semaphore_signal(barrier, inc=1, device_id=target, device_id_type=pl.DeviceIdType.MESH)

    def greet_peer(off, _):
        greet({"vtx": lax.rem(me + off, peers)})
        return 0

    lax.fori_loop(1, peers, greet_peer, 0)

    def greet_far(q, _):
        greet({"vtx": 2 * q + core, "edg": z + 2 - 4 * half})
        return 0

    lax.fori_loop(0, peers // 2, greet_far, 0)

    @pl.when(z > 0)
    def _():
        greet({"edg": z - 1})

    @pl.when(z < 3)
    def _():
        greet({"edg": z + 1})

    @pl.when(lax.rem(u, 2) == 1)
    def _():
        greet({"vtx": me + 1 - 2 * core, "edg": mirrored(u - 1)})

    @pl.when(moves)
    def _():
        greet(swap_with)

    greeted = peers - 1 + peers // 2 + lax.rem(u, 2) + jnp.where(moves, 1, 0)
    greeted += jnp.where(z > 0, 1, 0) + jnp.where(z < 3, 1, 0)

    shape = (wide_rows, LANES)
    position = lax.broadcasted_iota(i32, shape, 0) * LANES + lax.broadcasted_iota(i32, shape, 1)
    live = position < count_ref[0]
    src, dst = src_ref[...], dst_ref[...]
    slots = dst - num_rows
    weight = jnp.where(live, weight_ref[...], 0.0)
    apart = jnp.logical_and(live, src != dst)
    held[...] = jnp.where(apart, weight_ref[...], 0.0)
    root = jnp.sqrt(held[...])
    list8[...] = jnp.full(list8.shape, -1, i32)
    list8[:peers, :slot] = list_ref[...]

    def swaps():
        pairs_of = [(src_ref, new_src), (dst_ref, new_dst), (held, new_held), (list8, new_list), (ground_ref, new_ground)]
        return [remote(a, b, swap_sem.at[0, i], swap_sem.at[1, i], swap_with) for i, (a, b) in enumerate(pairs_of)]

    @pl.when(stays)
    def _():
        new_src[...] = src_ref[...]
        new_dst[...] = dst_ref[...]
        new_held[...] = held[...]
        new_list[...] = list8[...]
        new_ground[...] = ground_ref[...]

    mask[...] = jnp.where(apart, 1.0, 0.0)
    peer_of = jnp.where(slots < 0, -1, slots // slot)
    within = jnp.where(slots < 0, -1, slots % slot)
    for k in range(wide_rows):
        cols = slice(k * LANES, (k + 1) * LANES)
        rowf[0:1, cols] = src[k : k + 1, :]
        rowf[1:2, cols] = dst[k : k + 1, :]
        rowf[2:3, cols] = peer_of[k : k + 1, :]
        rowf[3:4, cols] = within[k : k + 1, :]
        wide[0:1, cols] = weight[k : k + 1, :]

    root_t = root.T
    for k in range(wide_rows):
        rows = slice(k * LANES, (k + 1) * LANES)
        flows[rows, :] = pair(-(root_t[:, k : k + 1] * sketch_ref[rows, :].astype(f32)))

    def spread_columns():
        for values, store in ((new_src, srcb), (new_dst, dstb), (new_held, wb)):
            turned = values[...].T
            for k in range(wide_rows):
                rows = slice(k * LANES, (k + 1) * LANES)
                store[rows, :] = jnp.broadcast_to(turned[:, k : k + 1], (LANES, LANES)).astype(store.dtype)
        for k in range(wide_rows):
            cols = slice(k * LANES, (k + 1) * LANES)
            rowf[4:5, cols] = new_src[k : k + 1, :]
            rowf[5:6, cols] = new_dst[k : k + 1, :]
        spread_lists(new_list, 1)
        for ref in (res, dirn, sol, part):
            ref[...] = jnp.zeros(ref.shape, f32)

    def count_up(rows, up_at, low, weights):
        edges = weights.shape[1]
        up = lax.broadcasted_iota(i32, (rows, edges), 0)
        picked = jnp.where(up == up_at, weights, 0.0)
        parts = dot_lanes(jnp.concatenate(split3(picked), axis=0), one_hot(down_rows(low, 0, LANES)))
        return parts[:rows] + parts[rows : 2 * rows] + parts[2 * rows :]

    def degree_of(to):
        return degh.at[to]

    def far_degree():
        got = count_up(-(-peers // 16) * 16, rowf[2:3, :], rowf[3:4, :], wide[0:1, :num_edges])
        for q in range(peers):
            degh[q] = jnp.broadcast_to(got[q : q + 1, :], (8, LANES))
        exchange(at_home, degree_of, dback, deg_sem.at[0], deg_sem.at[1])
        dback[me] = degh[me]

    def spread_lists(lists, row):
        list_t = lists[...].T
        for q in range(peers):
            listb[q * slot : (q + 1) * slot, :] = jnp.broadcast_to(list_t[:, q : q + 1], (LANES, LANES))[:slot]
        for at in range(0, halo_len, LANES):
            listrow[row : row + 1, at : at + LANES] = listb[at : at + LANES, :].T[0:1, :]

    def scatter_rows(at, rows, edges):
        acc[:rows, :] = jnp.zeros((rows, 2 * columns), f32)

        def body(k, _):
            cols = pl.ds(pl.multiple_of(k * ktile, ktile), ktile)
            pick = signed(down_rows(rowf[edges : edges + 1, cols], at, rows), down_rows(rowf[edges + 1 : edges + 2, cols], at, rows))
            acc[:rows, :] += dot(pick, flows[cols, :])
            return 0

        lax.fori_loop(0, num_edges // ktile, body, 0)
        return halves(acc[:rows, :])

    def edge_hots(rows, at, width):
        hots = zip(along_lanes(srcb[rows, :], at, width), along_lanes(dstb[rows, :], at, width))
        return jnp.concatenate([signed(a, b) for a, b in hots], axis=1)

    def gather_near(group, q, tail=False):
        for off in range(0, quarter, etile):
            rows = pl.ds(pl.multiple_of(q * quarter + off, etile), etile)
            base = pl.multiple_of(group * GROUP, GROUP)
            hots = edge_hots(rows, base, GROUP)
            got = part[rows, :] + halves(dot(hots, field[pl.ds(base, GROUP), :]))
            part[rows, :] = got
            if tail:
                flows[rows, :] = pair(got * wb[rows, :])

    def own_degree():
        rows = -(-high // 16) * 16
        got = jnp.zeros((rows, LANES), f32)
        for row in (0, 1):
            at = rowf[row : row + 1, :]
            got += count_up(rows, at // LANES, at % LANES, wide[0:1, :num_edges])
        for q in range(peers):
            list8row[0:1, q * LANES : (q + 1) * LANES] = list8[q : q + 1, :]
            wide[1:2, q * LANES : (q + 1) * LANES] = dback[q, 0:1, :]
        at = list8row[...]
        landing = count_up(rows, jnp.where(at < 0, -1, at // LANES), at % LANES, wide[1:2, : peers * LANES])
        degown[:high, :] = (got + landing)[:high]
        degown[high:, :] = landing[:high]

    def degree_copy(kind, land, src, dst, target):
        return remote(src, dst, degline_sem.at[0, kind], degline_sem.at[1, land], target)

    def degree_sum():
        return degree_copy(0, 0, degown, degouter, inward)

    def degree_part():
        return degree_copy(1, 1, degmine, deginner, inward)

    def degree_total(j):
        return degree_copy(2 + j, 2, degtotal, degtotal, totals_to[j])

    hpiece = even_piece(halo_len, 512)

    def back_of(s, place):
        def halo_of(to):
            return yhalo.at[s, pl.ds(pl.multiple_of(to * slot, 8), slot)]

        return place, halo_of, back.at[s], back_sem.at[0, s], back_sem.at[1, s]

    def send_back(s, place, edges):
        for at in range(0, halo_len, hpiece):
            yhalo[s, at : at + hpiece, :] = scatter_rows(num_rows + at, hpiece, edges)
        if edges == 0:
            pl.semaphore_wait(barrier, greeted)
        exchange(*back_of(s, place))
        back[s, place[0]] = yhalo[s, pl.ds(pl.multiple_of(place[0] * slot, 8), slot), :]

    send_back(0, at_home, 0)

    @pl.when(moves)
    def _():
        for copy in swaps():
            copy.start()

    far_degree()
    spread_lists(list8, 0)

    def piece_rows(k):
        return pl.ds(pl.multiple_of(k * PIECE, PIECE), PIECE)

    def line_copy(s, kind, land, k, src, dst, target):
        rows = piece_rows(k)
        return remote(
            src.at[s, rows], dst.at[s, rows], line_sem.at[0, s, kind, k], line_sem.at[1, s, land, k], target
        )

    def own_rows(s, c, place, edges):
        at = pl.multiple_of(c * GROUP, GROUP)
        local = scatter_rows(at, GROUP, edges)

        @pl.when(c == 0)
        def _():
            exchange_wait(*back_of(s, place))
            retb[...] = pair(back[s].reshape(halo_len, columns))

        pick = one_hot(down_rows(listrow[min(edges, 1) : min(edges, 1) + 1, :], at, GROUP))
        own[s, pl.ds(at, GROUP), :] = local + halves(dot(pick, retb[...]))

    def update(s, rows, keep, push, last):
        old = dirn[rows, :]
        residual = res[rows, :] - (groundb[rows, :] * old + total[s, rows, :])
        direction = keep * old + push * invb[rows, :] * residual
        shown = sol[rows, :] + direction
        res[rows, :] = residual
        dirn[rows, :] = direction
        sol[rows, :] = shown
        field[rows, :] = pair(jnp.where(last, shown, direction))

    def pick_group(s, group):
        base = pl.multiple_of(group * GROUP, GROUP)
        for at in range(0, halo_len, hpiece):
            spread = listb[at : at + hpiece, :].astype(jnp.int16)
            hots = jnp.concatenate([one_hot(m) for m in along_lanes(spread, base, GROUP)], axis=1)
            got = halves(dot(hots, field[pl.ds(base, GROUP), :]))
            listed[s, at : at + hpiece, :] = jnp.where(group == 0, got, listed[s, at : at + hpiece, :] + got)

    def sum_at_home(keep, push, last):
        def to_inward(k):
            return line_copy(0, 0, 0, k, own, outer, inward)

        def part_inward(k):
            return line_copy(0, 1, 1, k, mine, inner, inward)

        def give_total(k, j):
            return line_copy(0, 2 + j, 2, k, total, total, totals_to[j])

        def pass_partial(k):
            rows = piece_rows(k)
            to_inward(k).wait_recv()
            mine[0, rows, :] = own[0, rows, :] + outer[0, rows, :]
            part_inward(k).start()

        sends = jnp.logical_or(u == 0, u == 3)

        def group_rows(c, _):
            own_rows(0, c, at_home, 0)

            @pl.when(sends)
            def _():
                for j in range(per):
                    to_inward(c * per + j).start()

            @pl.when(c == 0)
            def _():
                exchange_wait(at_home, degree_of, dback, deg_sem.at[0], deg_sem.at[1])
                own_degree()

                @pl.when(sends)
                def _():
                    degree_sum().start()

                @pl.when(moves)
                def _():
                    for copy in swaps():
                        copy.wait()

                spread_columns()

            @pl.when(jnp.logical_and(u == 2, c == groups - 2))
            def _():
                degree_sum().wait_recv()
                degmine[...] = degown[...] + degouter[...]
                degree_part().start()
                for k in range(LAG):
                    pass_partial(k)

            return 0

        lax.fori_loop(0, groups, group_rows, 0)

        @pl.when(u == 1)
        def _():
            degree_sum().wait_recv()
            degree_part().wait_recv()
            degtotal[...] = (degown[...] + degouter[...]) + deginner[...]
            for j in range(3):
                degree_total(j).start()

        @pl.when(u != 1)
        def _():
            degree_total(0).wait_recv()

        inverse_t = (1.0 / (degtotal[:high, :] + new_ground[...])).T
        held_t = (degtotal[high:, :] + new_ground[...]).T
        for j in range(high):
            rows = slice(j * LANES, (j + 1) * LANES)
            invb[rows, :] = jnp.broadcast_to(inverse_t[:, j : j + 1], (LANES, LANES))
            groundb[rows, :] = jnp.broadcast_to(held_t[:, j : j + 1], (LANES, LANES))

        def step(k, _):
            rows = piece_rows(k)

            @pl.when(jnp.logical_and(u == 2, k + LAG < count))
            def _():
                pass_partial(k + LAG)

            @pl.when(u == 1)
            def _():
                to_inward(k).wait_recv()
                part_inward(k).wait_recv()
                total[0, rows, :] = (own[0, rows, :] + outer[0, rows, :]) + inner[0, rows, :]
                for j in range(3):
                    give_total(k, j).start()

            @pl.when(u != 1)
            def _():
                give_total(k, 0).wait_recv()

            update(0, rows, keep, push, last)
            group, j = k // per, lax.rem(k, per)

            @pl.when(j == per - 1)
            def _():
                pick_group(0, group)

            @pl.when(group > 0)
            def _():
                gather_near(group - 1, j)

            return 0

        lax.fori_loop(0, count, step, 0)

        def line_done(k, _):
            @pl.when(sends)
            def _():
                to_inward(k).wait_send()

            @pl.when(u == 2)
            def _():
                part_inward(k).wait_send()

            @pl.when(u == 1)
            def _():
                for j in range(3):
                    give_total(k, j).wait_send()

            return 0

        lax.fori_loop(0, count, line_done, 0)

        @pl.when(sends)
        def _():
            degree_sum().wait_send()

        @pl.when(u == 2)
        def _():
            degree_part().wait_send()

        @pl.when(u == 1)
        def _():
            for j in range(3):
                degree_total(j).wait_send()

    def show(m, held_in):
        rows = pl.ds(pl.multiple_of(m * 2 * PIECE, 2 * PIECE), 2 * PIECE)
        return remote(held_in.at[rows], sol_in.at[rows], sol_sem.at[0, m], sol_sem.at[1, m], outward)

    def first_show(m):
        return show(m, sol)

    def next_show(m):
        return show(m, sol_in)

    def forward(m):
        first_show(m).wait_recv()
        next_show(m).start()

    def sum_at_host(s, keep, push, last):
        def lend(k):
            return line_copy(s, 0, 0, k, own, outer, other_core)

        def cross(k):
            return line_copy(s, 1, 1, k, mine, inner, across)

        def share(k):
            return line_copy(s, 2, 2, k, total, total, other_core)

        def pair_sum(c):
            for j in range(per // 2):
                k = c * per + 2 * j + core
                rows = piece_rows(k)
                lend(k).wait_recv()
                mine[s, rows, :] = own[s, rows, :] + outer[s, rows, :]
                cross(k).start()

        def group_rows(c, _):
            own_rows(s, c, at_host, 4)
            for j in range(per // 2):
                lend(c * per + 2 * j + 1 - core).start()

            @pl.when(c > 0)
            def _():
                pair_sum(c - 1)

            return 0

        lax.fori_loop(0, groups, group_rows, 0)
        pair_sum(groups - 1)

        def step(m, _):
            k = 2 * m + core
            rows = piece_rows(k)
            cross(k).wait_recv()
            total[s, rows, :] = mine[s, rows, :] + inner[s, rows, :]
            share(k).start()
            share(2 * m + 1 - core).wait_recv()
            update(s, pl.ds(pl.multiple_of(m * 2 * PIECE, 2 * PIECE), 2 * PIECE), keep, push, last)

            @pl.when(jnp.logical_and(last, u == 1))
            def _():
                first_show(m).start()

            @pl.when(jnp.logical_and(jnp.logical_and(last, u == 2), m >= LEAD))
            def _():
                forward(m - LEAD)

            group, j = m // (per // 2), lax.rem(m, per // 2)

            @pl.when(j == per // 2 - 1)
            def _():
                pick_group(s, group)

            @pl.when(group > 0)
            def _():
                gather_near(group - 1, 2 * j)
                gather_near(group - 1, 2 * j + 1)

            return 0

        lax.fori_loop(0, count // 2, step, 0)

        def sent(m, _):
            lend(2 * m + 1 - core).wait_send()
            cross(2 * m + core).wait_send()
            share(2 * m + core).wait_send()
            return 0

        lax.fori_loop(0, count // 2, sent, 0)

    def stage(s, _):
        begin, last = s == 0, s == ITERS - 1
        keep, push = jnp.float32(0.0), jnp.float32(first)
        for at, (k_coef, p_coef) in enumerate(pairs):
            keep = jnp.where(s == at + 1, jnp.float32(k_coef), keep)
            push = jnp.where(s == at + 1, jnp.float32(p_coef), push)

        @pl.when(begin)
        def _():
            sum_at_home(keep, push, last)

        @pl.when(jnp.logical_not(begin))
        def _():
            sum_at_host(s, keep, push, last)

        def listed_of(to):
            return listed.at[s, pl.ds(pl.multiple_of(to * slot, 8), slot)]

        land_args = (at_host, listed_of, landed.at[s], land_sem.at[0, s], land_sem.at[1, s])
        exchange(*land_args)
        landed[s, block] = listed[s, pl.ds(pl.multiple_of(block * slot, 8), slot), :]

        def near_tail(q, _):
            gather_near(groups - 1, q, True)
            return 0

        lax.fori_loop(0, 4, near_tail, 0)

        @pl.when(jnp.logical_not(last))
        def _():
            send_back(s + 1, at_host, 4)

        @pl.when(jnp.logical_and(last, u == 2))
        def _():
            for m in range(count // 2 - LEAD, count // 2):
                forward(m)

        exchange_wait(*land_args)
        field[num_rows:, :] = pair(landed[s].reshape(halo_len, columns))

        def gather_far(k):
            rows = pl.ds(pl.multiple_of(k * etile, etile), etile)
            gap = part[rows, :] + halves(dot(edge_hots(rows, num_rows, halo_len), field[num_rows:, :]))
            part[rows, :] = jnp.zeros(gap.shape, f32)
            return rows, gap

        @pl.when(jnp.logical_not(last))
        def _():
            def make_flows(k, _):
                rows, gap = gather_far(k)
                flows[rows, :] = pair(gap * wb[rows, :])
                return 0

            lax.fori_loop(0, num_edges // etile, make_flows, 0)

        @pl.when(last)
        def _():
            def make_gaps(k, _):
                rows, gap = gather_far(k)
                square = gap * gap
                for i in range(etile // LANES):
                    turned = square[i * LANES : (i + 1) * LANES, :].T
                    row = pl.ds(k * (etile // LANES) + i, 1)
                    gaps[row, :] = jnp.sum(turned, axis=0, keepdims=True)
                return 0

            lax.fori_loop(0, num_edges // etile, make_gaps, 0)

        return 0

    lax.fori_loop(0, ITERS, stage, 0)

    def gaps_home():
        return remote(gaps, gaps_in, swap_sem.at[0, 5], swap_sem.at[1, 5], swap_with)

    @pl.when(stays)
    def _():
        out_ref[...] = sol[...]
        gap_ref[...] = mask[...] * gaps[...] / columns

    @pl.when(moves)
    def _():
        gaps_home().start()

    @pl.when(u == 3)
    def _():
        for m in range(count // 2):
            first_show(m).wait_recv()

    @pl.when(jnp.logical_or(u == 1, u == 2))
    def _():
        for m in range(count // 2):
            first_show(m).wait_send()

    @pl.when(moves)
    def _():
        out_ref[...] = sol_in[...]
        gaps_home().wait()
        gap_ref[...] = mask[...] * gaps_in[...] / columns


def local(sketch_cols, edge_weight, ground, src_local, dst_index, send_rows, edge_count):
    peers = lax.axis_size("vtx")
    num_rows, num_edges = ground.shape[0], edge_weight.shape[0]
    slot, columns = send_rows.shape[2], sketch_cols.shape[1]
    halo_len, high, wide_rows = peers * slot, num_rows // LANES, num_edges // LANES
    count = num_rows // PIECE
    f32, bf16, i32, i16 = jnp.float32, jnp.bfloat16, jnp.int32, jnp.int16
    vmem, dma = pltpu.VMEM, pltpu.SemaphoreType.DMA
    peers8 = -(-peers // 8) * 8
    halo = vmem((ITERS, peers, slot, columns), f32)
    flat_halo = vmem((ITERS, halo_len, columns), f32)
    rows_f32 = vmem((num_rows, columns), f32)
    line = vmem((ITERS, num_rows, columns), f32)
    small = vmem((2 * high, LANES), f32)
    spread = vmem((num_edges, LANES), i16)
    wide_f32 = vmem((wide_rows, LANES), f32)
    scratch = [
        vmem((8, num_edges), i32), spread, spread,
        vmem((8, max(num_edges, peers * LANES)), f32), vmem((num_edges, LANES), f32),
        vmem((halo_len, LANES), i32), vmem((2, halo_len), i32),
        rows_f32, rows_f32, rows_f32, rows_f32, rows_f32,
        vmem((num_rows + halo_len, 2 * columns), bf16), vmem((num_edges, columns), f32),
        vmem((GROUP, 2 * columns), f32), vmem((halo_len, 2 * columns), bf16),
        vmem((num_edges, 2 * columns), bf16), line, line, line, line, line,
        flat_halo, halo, flat_halo, halo,
        vmem((wide_rows, LANES), f32), vmem((peers8, LANES), i32),
        vmem((1, peers * LANES), i32),
        small, small, small, small, small, vmem((peers, 8, LANES), f32), vmem((peers, 8, LANES), f32),
        vmem((wide_rows, LANES), i32), vmem((wide_rows, LANES), i32), wide_f32, wide_f32,
        vmem((peers8, LANES), i32), vmem((high, LANES), f32), wide_f32, wide_f32, rows_f32,
        dma((2, ITERS, peers)), dma((2, ITERS, peers)), dma((2, peers)), dma((2, ITERS, 5, count)), dma((2, 5)),
        dma((2, 6)), dma((2, count // 2)),
    ]
    in_vmem = pl.BlockSpec(memory_space=pltpu.VMEM)
    solution, gaps = pl.pallas_call(
        functools.partial(kernel, peers),
        in_specs=[in_vmem] * 6 + [pl.BlockSpec(memory_space=pltpu.SMEM)],
        out_specs=[in_vmem] * 2,
        out_shape=[jax.ShapeDtypeStruct((num_rows, columns), f32), jax.ShapeDtypeStruct((wide_rows, LANES), f32)],
        scratch_shapes=scratch,
        compiler_params=pltpu.CompilerParams(collective_id=0, has_side_effects=True, vmem_limit_bytes=VMEM_LIMIT),
        name="sketch",
    )(
        sketch_cols, edge_weight.reshape(wide_rows, LANES), ground.reshape(high, LANES),
        src_local.reshape(wide_rows, LANES), dst_index.reshape(wide_rows, LANES), send_rows[0], edge_count,
    )
    return solution, gaps.reshape(-1)


def solution(mesh):
    in_specs = (
        P(("vtx", "edg"), None),
        P(("vtx", "edg")),
        P("vtx"),
        P(("vtx", "edg")),
        P(("vtx", "edg")),
        P(("vtx", "edg"), None, None),
        P(("vtx", "edg")),
    )
    out_specs = (P("vtx", None), P(("vtx", "edg")))
    return jax.shard_map(local, mesh=mesh, in_specs=in_specs, out_specs=out_specs, check_vma=False)
```

```python
import functools

import jax
import jax.numpy as jnp
from jax import lax
from jax.experimental import pallas as pl
from jax.experimental.pallas import tpu as pltpu
from jax.sharding import PartitionSpec as P

ITERS = 3

lam_low = 0.05
lam_high = 2.0
LANES = 128
VMEM_LIMIT = 65600000
GROUP = 512
HOST_GROUP = 512
HOME_GROUP = 512
PIECE = 128
LAG = 4
LEAD = 2


def chebyshev_terms(steps):
    centre = (lam_high + lam_low) / 2.0
    half_width = (lam_high - lam_low) / 2.0
    sigma_val = centre / half_width
    rho_prev = 1.0 / sigma_val
    pairs = []
    for count_idx in range(steps - 1):
        rho_next = 1.0 / (2.0 * sigma_val - rho_prev)
        pairs.append((rho_next * rho_prev, 2.0 * rho_next / half_width))
        rho_prev = rho_next
    return (1.0 / centre, pairs)


def split2(x):
    hi = x.astype(jnp.bfloat16)
    lo = (x - hi.astype(jnp.float32)).astype(jnp.bfloat16)
    return hi, lo


def split3(x):
    hi = x.astype(jnp.bfloat16)
    rest = x - hi.astype(jnp.float32)
    mid, lo = split2(rest)
    return hi, mid, lo


def pair(x):
    return jnp.concatenate(split2(x), axis=1)


def halves(x):
    n = x.shape[1] // 2
    return x[:, :n] + x[:, n:]


def dot(a, b):
    return jnp.dot(a, b, preferred_element_type=jnp.float32)


def dot_lanes(a, b):
    return lax.dot_general(a, b, (((1,), (1,)), ((), ())), preferred_element_type=jnp.float32)


def signed(is_src, is_dst):
    one, none = jnp.ones(is_src.shape, jnp.bfloat16), jnp.zeros(is_src.shape, jnp.bfloat16)
    return jnp.where(is_src, one, jnp.where(is_dst, -one, none))


def one_hot(match):
    return jnp.where(match, jnp.ones(match.shape, jnp.bfloat16), jnp.zeros(match.shape, jnp.bfloat16))


def short(x, shape):
    return jnp.broadcast_to(jnp.asarray(x, jnp.int32), shape).astype(jnp.int16)


def down_rows(row, at, rows):
    shape = (rows, row.shape[1])
    return lax.broadcasted_iota(jnp.int16, shape, 0) == jnp.broadcast_to((row - at).astype(jnp.int16), shape)


def along_lanes(spread, at, width):
    parts = []
    lane = lax.broadcasted_iota(jnp.int16, spread.shape, 1)
    for off in range(0, width, LANES):
        parts.append(lane + short(at + off, spread.shape) == spread)
    return parts


def even_piece(total, most):
    return max(n for n in range(8, most + 1, 8) if total % n == 0)


def remote(src, dst, send_sem, recv_sem, target):
    return pltpu.make_async_remote_copy(
        src_ref=src, dst_ref=dst, send_sem=send_sem, recv_sem=recv_sem,
        device_id=target, device_id_type=pl.DeviceIdType.MESH,
    )


def exchange(place, src, dst, send_sem, recv_sem):
    me, peers, target = place

    def start(off, _):
        to = lax.rem(me + off, peers)
        remote(src(to), dst.at[me], send_sem.at[off], recv_sem.at[off], target(to)).start()
        return 0

    lax.fori_loop(0, peers // 2, lambda i, _: start(2 * i + 1, _), 0)
    lax.fori_loop(1, peers // 2, lambda i, _: start(2 * i, _), 0)


def exchange_wait(place, src, dst, send_sem, recv_sem):
    me, peers, target = place

    def wait(off, _):
        to = lax.rem(me + off, peers)
        origin = lax.rem(me + peers - off, peers)
        remote(src(to), dst.at[origin], send_sem.at[off], recv_sem.at[off], target(to)).wait()
        return 0

    lax.fori_loop(1, peers, wait, 0)


def kernel(
    peers, sketch_ref, weight_ref, ground_ref, src_ref, dst_ref, list_ref, count_ref, out_ref, gap_ref,
    rowf, srcb, dstb, wide, wb, listb, listrow, groundb, invb, res, dirn, sol, field, part, acc, retb,
    flows, own, outer, inner, mine, total, yhalo, back, listed, landed, mask, list8, list8row,
    degown, degouter, deginner, degmine, degtotal, degh, dback,
    new_src, new_dst, held, new_held, new_list, new_ground, gaps, gaps_in, sol_in,
    back_sem, land_sem, deg_sem, line_sem, degline_sem, swap_sem, sol_sem,
):
    first, pairs = chebyshev_terms(ITERS)
    me, z = lax.axis_index("vtx"), lax.axis_index("edg")
    slot, columns = back.shape[2], back.shape[3]
    halo_len = peers * slot
    wide_rows = src_ref.shape[0]
    num_edges = wide_rows * LANES
    num_rows = out_ref.shape[0]
    high = num_rows // LANES
    ktile = min(2048, num_edges)
    etile = 1024
    quarter = num_edges // 4
    groups = num_rows // GROUP
    host_groups, home_groups = num_rows // HOST_GROUP, num_rows // HOME_GROUP
    host_pairs = HOST_GROUP // PIECE // 2
    per = GROUP // PIECE
    count = num_rows // PIECE
    core, half = lax.rem(me, 2), z // 2

    def mirrored(at):
        return at + core * (3 - 2 * at)

    u = mirrored(z)
    moves = u >= 2
    stays = u < 2
    block = 2 * (me // 2) + half
    other_core = {"vtx": me + 1 - 2 * core}
    across = {"edg": z + 1 - 2 * lax.rem(z, 2)}
    swap_with = {"vtx": me + 1 - 2 * core, "edg": z + 2 - 4 * half}
    inward = {"edg": mirrored(jnp.where(u == 0, 1, u - 1))}
    totals_to = [other_core, {"edg": mirrored(0)}, {"vtx": me + 1 - 2 * core, "edg": mirrored(0)}]
    outward = {"edg": mirrored(jnp.where(u == 1, 2, 3))}

    def home(to):
        return {"vtx": to}

    def hosted(to):
        return {"vtx": 2 * (to // 2) + core, "edg": 2 * lax.rem(to, 2) + lax.rem(z, 2)}

    at_home, at_host = (me, peers, home), (block, peers, hosted)
    f32, bf16, i32 = jnp.float32, jnp.bfloat16, jnp.int32

    barrier = pltpu.get_barrier_semaphore()

    def greet(target):
        pl.semaphore_signal(barrier, inc=1, device_id=target, device_id_type=pl.DeviceIdType.MESH)

    def greet_peer(off, _):
        greet({"vtx": lax.rem(me + off, peers)})
        return 0

    lax.fori_loop(1, peers, greet_peer, 0)

    def greet_far(q, _):
        greet({"vtx": 2 * q + core, "edg": z + 2 - 4 * half})
        return 0

    lax.fori_loop(0, peers // 2, greet_far, 0)

    @pl.when(z > 0)
    def _():
        greet({"edg": z - 1})

    @pl.when(z < 3)
    def _():
        greet({"edg": z + 1})

    @pl.when(lax.rem(u, 2) == 1)
    def _():
        greet({"vtx": me + 1 - 2 * core, "edg": mirrored(u - 1)})

    @pl.when(moves)
    def _():
        greet(swap_with)

    greeted = peers - 1 + peers // 2 + lax.rem(u, 2) + jnp.where(moves, 1, 0)
    greeted += jnp.where(z > 0, 1, 0) + jnp.where(z < 3, 1, 0)

    shape = (wide_rows, LANES)
    position = lax.broadcasted_iota(i32, shape, 0) * LANES + lax.broadcasted_iota(i32, shape, 1)
    live = position < count_ref[0]
    src, dst = src_ref[...], dst_ref[...]
    slots = dst - num_rows
    weight = jnp.where(live, weight_ref[...], 0.0)
    apart = jnp.logical_and(live, src != dst)
    held[...] = jnp.where(apart, weight_ref[...], 0.0)
    root = jnp.sqrt(held[...])
    list8[...] = jnp.full(list8.shape, -1, i32)
    list8[:peers, :slot] = list_ref[...]

    def swaps():
        pairs_of = [(src_ref, new_src), (dst_ref, new_dst), (held, new_held), (list8, new_list), (ground_ref, new_ground)]
        return [remote(a, b, swap_sem.at[0, i], swap_sem.at[1, i], swap_with) for i, (a, b) in enumerate(pairs_of)]

    @pl.when(stays)
    def _():
        new_src[...] = src_ref[...]
        new_dst[...] = dst_ref[...]
        new_held[...] = held[...]
        new_list[...] = list8[...]
        new_ground[...] = ground_ref[...]

    mask[...] = jnp.where(apart, 1.0, 0.0)
    peer_of = jnp.where(slots < 0, -1, slots // slot)
    within = jnp.where(slots < 0, -1, slots % slot)
    for k in range(wide_rows):
        cols = slice(k * LANES, (k + 1) * LANES)
        rowf[0:1, cols] = src[k : k + 1, :]
        rowf[1:2, cols] = dst[k : k + 1, :]
        rowf[2:3, cols] = peer_of[k : k + 1, :]
        rowf[3:4, cols] = within[k : k + 1, :]
        wide[0:1, cols] = weight[k : k + 1, :]

    root_t = root.T
    for k in range(wide_rows):
        rows = slice(k * LANES, (k + 1) * LANES)
        flows[rows, :] = pair(-(root_t[:, k : k + 1] * sketch_ref[rows, :].astype(f32)))

    def spread_columns():
        for values, store in ((new_src, srcb), (new_dst, dstb), (new_held, wb)):
            turned = values[...].T
            for k in range(wide_rows):
                rows = slice(k * LANES, (k + 1) * LANES)
                store[rows, :] = jnp.broadcast_to(turned[:, k : k + 1], (LANES, LANES)).astype(store.dtype)
        for k in range(wide_rows):
            cols = slice(k * LANES, (k + 1) * LANES)
            rowf[4:5, cols] = new_src[k : k + 1, :]
            rowf[5:6, cols] = new_dst[k : k + 1, :]
        spread_lists(new_list, 1)
        for ref in (res, dirn, sol, part):
            ref[...] = jnp.zeros(ref.shape, f32)

    def count_up(rows, up_at, low, weights):
        edges = weights.shape[1]
        up = lax.broadcasted_iota(i32, (rows, edges), 0)
        picked = jnp.where(up == up_at, weights, 0.0)
        parts = dot_lanes(jnp.concatenate(split3(picked), axis=0), one_hot(down_rows(low, 0, LANES)))
        return parts[:rows] + parts[rows : 2 * rows] + parts[2 * rows :]

    def degree_of(to):
        return degh.at[to]

    def far_degree():
        got = count_up(-(-peers // 16) * 16, rowf[2:3, :], rowf[3:4, :], wide[0:1, :num_edges])
        for q in range(peers):
            degh[q] = jnp.broadcast_to(got[q : q + 1, :], (8, LANES))
        exchange(at_home, degree_of, dback, deg_sem.at[0], deg_sem.at[1])
        dback[me] = degh[me]

    def spread_lists(lists, row):
        list_t = lists[...].T
        for q in range(peers):
            listb[q * slot : (q + 1) * slot, :] = jnp.broadcast_to(list_t[:, q : q + 1], (LANES, LANES))[:slot]
        for at in range(0, halo_len, LANES):
            listrow[row : row + 1, at : at + LANES] = listb[at : at + LANES, :].T[0:1, :]

    def scatter_rows(at, rows, edges):
        acc[:rows, :] = jnp.zeros((rows, 2 * columns), f32)

        def body(k, _):
            cols = pl.ds(pl.multiple_of(k * ktile, ktile), ktile)
            pick = signed(down_rows(rowf[edges : edges + 1, cols], at, rows), down_rows(rowf[edges + 1 : edges + 2, cols], at, rows))
            acc[:rows, :] += dot(pick, flows[cols, :])
            return 0

        lax.fori_loop(0, num_edges // ktile, body, 0)
        return halves(acc[:rows, :])

    def edge_hots(rows, at, width):
        hots = zip(along_lanes(srcb[rows, :], at, width), along_lanes(dstb[rows, :], at, width))
        return jnp.concatenate([signed(a, b) for a, b in hots], axis=1)

    def gather_near(group, q, tail=False):
        for off in range(0, quarter, etile):
            rows = pl.ds(pl.multiple_of(q * quarter + off, etile), etile)
            base = pl.multiple_of(group * GROUP, GROUP)
            hots = edge_hots(rows, base, GROUP)
            got = part[rows, :] + halves(dot(hots, field[pl.ds(base, GROUP), :]))
            part[rows, :] = got
            if tail:
                flows[rows, :] = pair(got * wb[rows, :])

    def own_degree():
        rows = -(-high // 16) * 16
        got = jnp.zeros((rows, LANES), f32)
        for row in (0, 1):
            at = rowf[row : row + 1, :]
            got += count_up(rows, at // LANES, at % LANES, wide[0:1, :num_edges])
        for q in range(peers):
            list8row[0:1, q * LANES : (q + 1) * LANES] = list8[q : q + 1, :]
            wide[1:2, q * LANES : (q + 1) * LANES] = dback[q, 0:1, :]
        at = list8row[...]
        landing = count_up(rows, jnp.where(at < 0, -1, at // LANES), at % LANES, wide[1:2, : peers * LANES])
        degown[:high, :] = (got + landing)[:high]
        degown[high:, :] = landing[:high]

    def degree_copy(kind, land, src, dst, target):
        return remote(src, dst, degline_sem.at[0, kind], degline_sem.at[1, land], target)

    def degree_sum():
        return degree_copy(0, 0, degown, degouter, inward)

    def degree_part():
        return degree_copy(1, 1, degmine, deginner, inward)

    def degree_total(j):
        return degree_copy(2 + j, 2, degtotal, degtotal, totals_to[j])

    hpiece = even_piece(halo_len, 512)

    def back_of(s, place):
        def halo_of(to):
            return yhalo.at[s, pl.ds(pl.multiple_of(to * slot, 8), slot)]

        return place, halo_of, back.at[s], back_sem.at[0, s], back_sem.at[1, s]

    def send_back(s, place, edges):
        for at in range(0, halo_len, hpiece):
            yhalo[s, at : at + hpiece, :] = scatter_rows(num_rows + at, hpiece, edges)
        if edges == 0:
            pl.semaphore_wait(barrier, greeted)
        exchange(*back_of(s, place))
        back[s, place[0]] = yhalo[s, pl.ds(pl.multiple_of(place[0] * slot, 8), slot), :]

    send_back(0, at_home, 0)

    @pl.when(moves)
    def _():
        for copy in swaps():
            copy.start()

    far_degree()
    spread_lists(list8, 0)

    def piece_rows(k):
        return pl.ds(pl.multiple_of(k * PIECE, PIECE), PIECE)

    def line_copy(s, kind, land, k, src, dst, target):
        rows = piece_rows(k)
        return remote(
            src.at[s, rows], dst.at[s, rows], line_sem.at[0, s, kind, k], line_sem.at[1, s, land, k], target
        )

    def own_rows(s, c, place, edges, size):
        at = pl.multiple_of(c * size, size)
        local = scatter_rows(at, size, edges)

        @pl.when(c == 0)
        def _():
            exchange_wait(*back_of(s, place))
            retb[...] = pair(back[s].reshape(halo_len, columns))

        pick = one_hot(down_rows(listrow[min(edges, 1) : min(edges, 1) + 1, :], at, size))
        own[s, pl.ds(at, size), :] = local + halves(dot(pick, retb[...]))

    def update(s, rows, keep, push, last):
        old = dirn[rows, :]
        residual = res[rows, :] - (groundb[rows, :] * old + total[s, rows, :])
        direction = keep * old + push * invb[rows, :] * residual
        shown = sol[rows, :] + direction
        res[rows, :] = residual
        dirn[rows, :] = direction
        sol[rows, :] = shown
        field[rows, :] = pair(jnp.where(last, shown, direction))

    def pick_group(s, group):
        base = pl.multiple_of(group * GROUP, GROUP)
        for at in range(0, halo_len, hpiece):
            spread = listb[at : at + hpiece, :].astype(jnp.int16)
            hots = jnp.concatenate([one_hot(m) for m in along_lanes(spread, base, GROUP)], axis=1)
            got = halves(dot(hots, field[pl.ds(base, GROUP), :]))
            listed[s, at : at + hpiece, :] = jnp.where(group == 0, got, listed[s, at : at + hpiece, :] + got)

    def sum_at_home(keep, push, last):
        def to_inward(k):
            return line_copy(0, 0, 0, k, own, outer, inward)

        def part_inward(k):
            return line_copy(0, 1, 1, k, mine, inner, inward)

        def give_total(k, j):
            return line_copy(0, 2 + j, 2, k, total, total, totals_to[j])

        def pass_partial(k):
            rows = piece_rows(k)
            to_inward(k).wait_recv()
            mine[0, rows, :] = own[0, rows, :] + outer[0, rows, :]
            part_inward(k).start()

        sends = jnp.logical_or(u == 0, u == 3)

        def group_rows(c, _):
            own_rows(0, c, at_home, 0, HOME_GROUP)

            @pl.when(sends)
            def _():
                for j in range(HOME_GROUP // PIECE):
                    to_inward(c * (HOME_GROUP // PIECE) + j).start()

            @pl.when(c == 0)
            def _():
                exchange_wait(at_home, degree_of, dback, deg_sem.at[0], deg_sem.at[1])
                own_degree()

                @pl.when(sends)
                def _():
                    degree_sum().start()

            @pl.when(c == 1)
            def _():
                @pl.when(moves)
                def _():
                    for copy in swaps():
                        copy.wait()

                spread_columns()

            @pl.when(jnp.logical_and(u == 2, c == home_groups - 2))
            def _():
                degree_sum().wait_recv()
                degmine[...] = degown[...] + degouter[...]
                degree_part().start()
                for k in range(LAG):
                    pass_partial(k)

            return 0

        lax.fori_loop(0, home_groups, group_rows, 0)

        @pl.when(u == 1)
        def _():
            degree_sum().wait_recv()
            degree_part().wait_recv()
            degtotal[...] = (degown[...] + degouter[...]) + deginner[...]
            for j in range(3):
                degree_total(j).start()

        @pl.when(u != 1)
        def _():
            degree_total(0).wait_recv()

        inverse_t = (1.0 / (degtotal[:high, :] + new_ground[...])).T
        held_t = (degtotal[high:, :] + new_ground[...]).T
        for j in range(high):
            rows = slice(j * LANES, (j + 1) * LANES)
            invb[rows, :] = jnp.broadcast_to(inverse_t[:, j : j + 1], (LANES, LANES))
            groundb[rows, :] = jnp.broadcast_to(held_t[:, j : j + 1], (LANES, LANES))

        def step(k, _):
            rows = piece_rows(k)

            @pl.when(jnp.logical_and(u == 2, k + LAG < count))
            def _():
                pass_partial(k + LAG)

            @pl.when(u == 1)
            def _():
                to_inward(k).wait_recv()
                part_inward(k).wait_recv()
                total[0, rows, :] = (own[0, rows, :] + outer[0, rows, :]) + inner[0, rows, :]
                for j in range(3):
                    give_total(k, j).start()

            @pl.when(u != 1)
            def _():
                give_total(k, 0).wait_recv()

            update(0, rows, keep, push, last)
            group, j = k // per, lax.rem(k, per)

            @pl.when(j == per - 1)
            def _():
                pick_group(0, group)

            @pl.when(jnp.logical_and(group > 0, k < count - per // 2))
            def _():
                gather_near(group - 1, j)

            return 0

        lax.fori_loop(0, count, step, 0)

        def line_done(k, _):
            @pl.when(sends)
            def _():
                to_inward(k).wait_send()

            @pl.when(u == 2)
            def _():
                part_inward(k).wait_send()

            @pl.when(u == 1)
            def _():
                for j in range(3):
                    give_total(k, j).wait_send()

            return 0

        lax.fori_loop(0, count, line_done, 0)

        @pl.when(sends)
        def _():
            degree_sum().wait_send()

        @pl.when(u == 2)
        def _():
            degree_part().wait_send()

        @pl.when(u == 1)
        def _():
            for j in range(3):
                degree_total(j).wait_send()

    def show(m, held_in):
        rows = pl.ds(pl.multiple_of(m * 2 * PIECE, 2 * PIECE), 2 * PIECE)
        return remote(held_in.at[rows], sol_in.at[rows], sol_sem.at[0, m], sol_sem.at[1, m], outward)

    def first_show(m):
        return show(m, sol)

    def next_show(m):
        return show(m, sol_in)

    def forward(m):
        first_show(m).wait_recv()
        next_show(m).start()

    def sum_at_host(s, keep, push, last):
        def lend(k):
            return line_copy(s, 0, 0, k, own, outer, other_core)

        def cross(k):
            return line_copy(s, 1, 1, k, mine, inner, across)

        def share(k):
            return line_copy(s, 2, 2, k, total, total, other_core)

        def pair_sum(c):
            for j in range(host_pairs):
                k = (c * host_pairs + j) * 2 + core
                rows = piece_rows(k)
                lend(k).wait_recv()
                mine[s, rows, :] = own[s, rows, :] + outer[s, rows, :]
                cross(k).start()

        def group_rows(c, _):
            own_rows(s, c, at_host, 4, HOST_GROUP)
            for j in range(host_pairs):
                lend((c * host_pairs + j) * 2 + 1 - core).start()

            @pl.when(c > 0)
            def _():
                pair_sum(c - 1)

            return 0

        lax.fori_loop(0, host_groups, group_rows, 0)
        pair_sum(host_groups - 1)

        def step(m, _):
            k = 2 * m + core
            rows = piece_rows(k)
            cross(k).wait_recv()
            total[s, rows, :] = mine[s, rows, :] + inner[s, rows, :]
            share(k).start()
            group, j = m // (per // 2), lax.rem(m, per // 2)

            @pl.when(jnp.logical_and(group > 0, m < count // 2 - 1))
            def _():
                gather_near(group - 1, 2 * j)
                gather_near(group - 1, 2 * j + 1)

            share(2 * m + 1 - core).wait_recv()
            update(s, pl.ds(pl.multiple_of(m * 2 * PIECE, 2 * PIECE), 2 * PIECE), keep, push, last)

            @pl.when(jnp.logical_and(last, u == 1))
            def _():
                first_show(m).start()

            @pl.when(jnp.logical_and(jnp.logical_and(last, u == 2), m >= LEAD))
            def _():
                forward(m - LEAD)

            @pl.when(j == per // 2 - 1)
            def _():
                pick_group(s, group)

            return 0

        lax.fori_loop(0, count // 2, step, 0)

        def sent(m, _):
            lend(2 * m + 1 - core).wait_send()
            cross(2 * m + core).wait_send()
            share(2 * m + core).wait_send()
            return 0

        lax.fori_loop(0, count // 2, sent, 0)

    def stage(s, _):
        begin, last = s == 0, s == ITERS - 1
        keep, push = jnp.float32(0.0), jnp.float32(first)
        for at, (k_coef, p_coef) in enumerate(pairs):
            keep = jnp.where(s == at + 1, jnp.float32(k_coef), keep)
            push = jnp.where(s == at + 1, jnp.float32(p_coef), push)

        @pl.when(begin)
        def _():
            sum_at_home(keep, push, last)

        @pl.when(jnp.logical_not(begin))
        def _():
            sum_at_host(s, keep, push, last)

        def listed_of(to):
            return listed.at[s, pl.ds(pl.multiple_of(to * slot, 8), slot)]

        land_args = (at_host, listed_of, landed.at[s], land_sem.at[0, s], land_sem.at[1, s])
        exchange(*land_args)
        landed[s, block] = listed[s, pl.ds(pl.multiple_of(block * slot, 8), slot), :]

        def near_left(q, _):
            gather_near(groups - 2, q)
            return 0

        lax.fori_loop(per // 2, per, near_left, 0)

        def near_tail(q, _):
            gather_near(groups - 1, q, True)
            return 0

        lax.fori_loop(0, 4, near_tail, 0)

        @pl.when(jnp.logical_not(last))
        def _():
            send_back(s + 1, at_host, 4)

        @pl.when(jnp.logical_and(last, u == 2))
        def _():
            for m in range(count // 2 - LEAD, count // 2):
                forward(m)

        exchange_wait(*land_args)
        field[num_rows:, :] = pair(landed[s].reshape(halo_len, columns))

        def gather_far(k):
            rows = pl.ds(pl.multiple_of(k * etile, etile), etile)
            gap = part[rows, :] + halves(dot(edge_hots(rows, num_rows, halo_len), field[num_rows:, :]))
            part[rows, :] = jnp.zeros(gap.shape, f32)
            return rows, gap

        @pl.when(jnp.logical_not(last))
        def _():
            def make_flows(k, _):
                rows, gap = gather_far(k)
                flows[rows, :] = pair(gap * wb[rows, :])
                return 0

            lax.fori_loop(0, num_edges // etile, make_flows, 0)

        @pl.when(last)
        def _():
            def make_gaps(k, _):
                rows, gap = gather_far(k)
                square = gap * gap
                for i in range(etile // LANES):
                    turned = square[i * LANES : (i + 1) * LANES, :].T
                    row = pl.ds(k * (etile // LANES) + i, 1)
                    gaps[row, :] = jnp.sum(turned, axis=0, keepdims=True)
                return 0

            lax.fori_loop(0, num_edges // etile, make_gaps, 0)

        return 0

    lax.fori_loop(0, ITERS, stage, 0)

    def gaps_home():
        return remote(gaps, gaps_in, swap_sem.at[0, 5], swap_sem.at[1, 5], swap_with)

    @pl.when(stays)
    def _():
        out_ref[...] = sol[...]
        gap_ref[...] = mask[...] * gaps[...] / columns

    @pl.when(moves)
    def _():
        gaps_home().start()

    @pl.when(u == 3)
    def _():
        for m in range(count // 2):
            first_show(m).wait_recv()

    @pl.when(jnp.logical_or(u == 1, u == 2))
    def _():
        for m in range(count // 2):
            first_show(m).wait_send()

    @pl.when(moves)
    def _():
        out_ref[...] = sol_in[...]
        gaps_home().wait()
        gap_ref[...] = mask[...] * gaps_in[...] / columns


def local(sketch_cols, edge_weight, ground, src_local, dst_index, send_rows, edge_count):
    peers = lax.axis_size("vtx")
    num_rows, num_edges = ground.shape[0], edge_weight.shape[0]
    slot, columns = send_rows.shape[2], sketch_cols.shape[1]
    halo_len, high, wide_rows = peers * slot, num_rows // LANES, num_edges // LANES
    count = num_rows // PIECE
    f32, bf16, i32, i16 = jnp.float32, jnp.bfloat16, jnp.int32, jnp.int16
    vmem, dma = pltpu.VMEM, pltpu.SemaphoreType.DMA
    peers8 = -(-peers // 8) * 8
    halo = vmem((ITERS, peers, slot, columns), f32)
    flat_halo = vmem((ITERS, halo_len, columns), f32)
    rows_f32 = vmem((num_rows, columns), f32)
    line = vmem((ITERS, num_rows, columns), f32)
    small = vmem((2 * high, LANES), f32)
    spread = vmem((num_edges, LANES), i16)
    wide_f32 = vmem((wide_rows, LANES), f32)
    scratch = [
        vmem((8, num_edges), i32), spread, spread,
        vmem((8, max(num_edges, peers * LANES)), f32), vmem((num_edges, LANES), f32),
        vmem((halo_len, LANES), i32), vmem((2, halo_len), i32),
        rows_f32, rows_f32, rows_f32, rows_f32, rows_f32,
        vmem((num_rows + halo_len, 2 * columns), bf16), vmem((num_edges, columns), f32),
        vmem((max(512, GROUP, HOST_GROUP, HOME_GROUP), 2 * columns), f32), vmem((halo_len, 2 * columns), bf16),
        vmem((num_edges, 2 * columns), bf16), line, line, line, line, line,
        flat_halo, halo, flat_halo, halo,
        vmem((wide_rows, LANES), f32), vmem((peers8, LANES), i32),
        vmem((1, peers * LANES), i32),
        small, small, small, small, small, vmem((peers, 8, LANES), f32), vmem((peers, 8, LANES), f32),
        vmem((wide_rows, LANES), i32), vmem((wide_rows, LANES), i32), wide_f32, wide_f32,
        vmem((peers8, LANES), i32), vmem((high, LANES), f32), wide_f32, wide_f32, rows_f32,
        dma((2, ITERS, peers)), dma((2, ITERS, peers)), dma((2, peers)), dma((2, ITERS, 5, count)), dma((2, 5)),
        dma((2, 6)), dma((2, count // 2)),
    ]
    in_vmem = pl.BlockSpec(memory_space=pltpu.VMEM)
    solution, gaps = pl.pallas_call(
        functools.partial(kernel, peers),
        in_specs=[in_vmem] * 6 + [pl.BlockSpec(memory_space=pltpu.SMEM)],
        out_specs=[in_vmem] * 2,
        out_shape=[pltpu.VMEM((num_rows, columns), f32), pltpu.VMEM((wide_rows, LANES), f32)],
        scratch_shapes=scratch,
        compiler_params=pltpu.CompilerParams(collective_id=0, has_side_effects=True, vmem_limit_bytes=VMEM_LIMIT),
        name="sketch",
    )(
        sketch_cols, edge_weight.reshape(wide_rows, LANES), ground.reshape(high, LANES),
        src_local.reshape(wide_rows, LANES), dst_index.reshape(wide_rows, LANES), send_rows[0], edge_count,
    )
    return solution, gaps.reshape(-1)


def solution(mesh):
    in_specs = (
        P(("vtx", "edg"), None),
        P(("vtx", "edg")),
        P("vtx"),
        P(("vtx", "edg")),
        P(("vtx", "edg")),
        P(("vtx", "edg"), None, None),
        P(("vtx", "edg")),
    )
    out_specs = (P("vtx", None), P(("vtx", "edg")))
    return jax.shard_map(local, mesh=mesh, in_specs=in_specs, out_specs=out_specs, check_vma=False)
```

```python
import functools

import jax
import jax.numpy as jnp
from jax import lax
from jax.experimental import pallas as pl
from jax.experimental.pallas import tpu as pltpu
from jax.sharding import PartitionSpec as P

ITERS = 3

lam_low = 0.05
lam_high = 2.0
LANES = 128
VMEM_LIMIT = 65600000
GROUP = 512
HOST_GROUP = 512
HOME_GROUP = 512
PIECE = 128
LAG = 8
HOLD = 1
LEAD = 2


def chebyshev_terms(steps):
    centre = (lam_high + lam_low) / 2.0
    half_width = (lam_high - lam_low) / 2.0
    sigma_val = centre / half_width
    rho_prev = 1.0 / sigma_val
    pairs = []
    for count_idx in range(steps - 1):
        rho_next = 1.0 / (2.0 * sigma_val - rho_prev)
        pairs.append((rho_next * rho_prev, 2.0 * rho_next / half_width))
        rho_prev = rho_next
    return (1.0 / centre, pairs)


def split2(x):
    hi = x.astype(jnp.bfloat16)
    lo = (x - hi.astype(jnp.float32)).astype(jnp.bfloat16)
    return hi, lo


def split3(x):
    hi = x.astype(jnp.bfloat16)
    rest = x - hi.astype(jnp.float32)
    mid, lo = split2(rest)
    return hi, mid, lo


def pair(x):
    return jnp.concatenate(split2(x), axis=1)


def halves(x):
    n = x.shape[1] // 2
    return x[:, :n] + x[:, n:]


def dot(a, b):
    return jnp.dot(a, b, preferred_element_type=jnp.float32)


def dot_lanes(a, b):
    return lax.dot_general(a, b, (((1,), (1,)), ((), ())), preferred_element_type=jnp.float32)


def signed(is_src, is_dst):
    one, none = jnp.ones(is_src.shape, jnp.bfloat16), jnp.zeros(is_src.shape, jnp.bfloat16)
    return jnp.where(is_src, one, jnp.where(is_dst, -one, none))


def one_hot(match):
    return jnp.where(match, jnp.ones(match.shape, jnp.bfloat16), jnp.zeros(match.shape, jnp.bfloat16))


def short(x, shape):
    return jnp.broadcast_to(jnp.asarray(x, jnp.int32), shape).astype(jnp.int16)


def down_rows(row, at, rows):
    shape = (rows, row.shape[1])
    return lax.broadcasted_iota(jnp.int16, shape, 0) == jnp.broadcast_to((row - at).astype(jnp.int16), shape)


def along_lanes(spread, at, width):
    parts = []
    lane = lax.broadcasted_iota(jnp.int16, spread.shape, 1)
    for off in range(0, width, LANES):
        parts.append(lane + short(at + off, spread.shape) == spread)
    return parts


def even_piece(total, most):
    return max(n for n in range(8, most + 1, 8) if total % n == 0)


def remote(src, dst, send_sem, recv_sem, target):
    return pltpu.make_async_remote_copy(
        src_ref=src, dst_ref=dst, send_sem=send_sem, recv_sem=recv_sem,
        device_id=target, device_id_type=pl.DeviceIdType.MESH,
    )


def exchange(place, src, dst, send_sem, recv_sem):
    me, peers, target = place

    def start(off, _):
        to = lax.rem(me + off, peers)
        remote(src(to), dst.at[me], send_sem.at[off], recv_sem.at[off], target(to)).start()
        return 0

    lax.fori_loop(0, peers // 2, lambda i, _: start(2 * i + 1, _), 0)
    lax.fori_loop(1, peers // 2, lambda i, _: start(2 * i, _), 0)


def exchange_wait(place, src, dst, send_sem, recv_sem):
    me, peers, target = place

    def wait(off, _):
        to = lax.rem(me + off, peers)
        origin = lax.rem(me + peers - off, peers)
        remote(src(to), dst.at[origin], send_sem.at[off], recv_sem.at[off], target(to)).wait()
        return 0

    lax.fori_loop(1, peers, wait, 0)


def kernel(
    peers, sketch_ref, weight_ref, ground_ref, src_ref, dst_ref, list_ref, count_ref, out_ref, gap_ref,
    rowf, srcb, dstb, wide, wb, listb, listrow, groundb, invb, res, dirn, sol, field, part, acc, retb,
    flows, own, outer, inner, mine, total, yhalo, back, listed, landed, mask, list8, list8row,
    degown, degouter, deginner, degmine, degtotal, degh, dback,
    new_src, new_dst, held, new_held, new_list, new_ground, gaps, gaps_in, sol_in,
    back_sem, land_sem, deg_sem, line_sem, degline_sem, swap_sem, sol_sem,
):
    first, pairs = chebyshev_terms(ITERS)
    me, z = lax.axis_index("vtx"), lax.axis_index("edg")
    slot, columns = back.shape[2], back.shape[3]
    halo_len = peers * slot
    wide_rows = src_ref.shape[0]
    num_edges = wide_rows * LANES
    num_rows = out_ref.shape[0]
    high = num_rows // LANES
    ktile = min(2048, num_edges)
    etile = 1024
    quarter = num_edges // 4
    groups = num_rows // GROUP
    host_groups, home_groups = num_rows // HOST_GROUP, num_rows // HOME_GROUP
    host_pairs = HOST_GROUP // PIECE // 2
    per = GROUP // PIECE
    count = num_rows // PIECE
    core, half = lax.rem(me, 2), z // 2

    def mirrored(at):
        return at + core * (3 - 2 * at)

    u = mirrored(z)
    moves = u >= 2
    stays = u < 2
    block = 2 * (me // 2) + half
    other_core = {"vtx": me + 1 - 2 * core}
    across = {"edg": z + 1 - 2 * lax.rem(z, 2)}
    swap_with = {"vtx": me + 1 - 2 * core, "edg": z + 2 - 4 * half}
    inward = {"edg": mirrored(jnp.where(u == 0, 1, u - 1))}
    totals_to = [other_core, {"edg": mirrored(0)}, {"vtx": me + 1 - 2 * core, "edg": mirrored(0)}]
    outward = {"edg": mirrored(jnp.where(u == 1, 2, 3))}

    def home(to):
        return {"vtx": to}

    def hosted(to):
        return {"vtx": 2 * (to // 2) + core, "edg": 2 * lax.rem(to, 2) + lax.rem(z, 2)}

    at_home, at_host = (me, peers, home), (block, peers, hosted)
    f32, bf16, i32 = jnp.float32, jnp.bfloat16, jnp.int32

    barrier = pltpu.get_barrier_semaphore()

    def greet(target):
        pl.semaphore_signal(barrier, inc=1, device_id=target, device_id_type=pl.DeviceIdType.MESH)

    def greet_peer(off, _):
        greet({"vtx": lax.rem(me + off, peers)})
        return 0

    lax.fori_loop(1, peers, greet_peer, 0)

    def greet_far(q, _):
        greet({"vtx": 2 * q + core, "edg": z + 2 - 4 * half})
        return 0

    lax.fori_loop(0, peers // 2, greet_far, 0)

    @pl.when(z > 0)
    def _():
        greet({"edg": z - 1})

    @pl.when(z < 3)
    def _():
        greet({"edg": z + 1})

    @pl.when(lax.rem(u, 2) == 1)
    def _():
        greet({"vtx": me + 1 - 2 * core, "edg": mirrored(u - 1)})

    @pl.when(moves)
    def _():
        greet(swap_with)

    greeted = peers - 1 + peers // 2 + lax.rem(u, 2) + jnp.where(moves, 1, 0)
    greeted += jnp.where(z > 0, 1, 0) + jnp.where(z < 3, 1, 0)

    shape = (wide_rows, LANES)
    position = lax.broadcasted_iota(i32, shape, 0) * LANES + lax.broadcasted_iota(i32, shape, 1)
    live = position < count_ref[0]
    src, dst = src_ref[...], dst_ref[...]
    slots = dst - num_rows
    weight = jnp.where(live, weight_ref[...], 0.0)
    apart = jnp.logical_and(live, src != dst)
    held[...] = jnp.where(apart, weight_ref[...], 0.0)
    root = jnp.sqrt(held[...])
    list8[...] = jnp.full(list8.shape, -1, i32)
    list8[:peers, :slot] = list_ref[...]

    def swaps():
        pairs_of = [(src_ref, new_src), (dst_ref, new_dst), (held, new_held), (list8, new_list), (ground_ref, new_ground)]
        return [remote(a, b, swap_sem.at[0, i], swap_sem.at[1, i], swap_with) for i, (a, b) in enumerate(pairs_of)]

    @pl.when(stays)
    def _():
        new_src[...] = src_ref[...]
        new_dst[...] = dst_ref[...]
        new_held[...] = held[...]
        new_list[...] = list8[...]
        new_ground[...] = ground_ref[...]

    mask[...] = jnp.where(apart, 1.0, 0.0)
    peer_of = jnp.where(slots < 0, -1, slots // slot)
    within = jnp.where(slots < 0, -1, slots % slot)
    for k in range(wide_rows):
        cols = slice(k * LANES, (k + 1) * LANES)
        rowf[0:1, cols] = src[k : k + 1, :]
        rowf[1:2, cols] = dst[k : k + 1, :]
        rowf[2:3, cols] = peer_of[k : k + 1, :]
        rowf[3:4, cols] = within[k : k + 1, :]
        wide[0:1, cols] = weight[k : k + 1, :]

    root_t = root.T
    for k in range(wide_rows):
        rows = slice(k * LANES, (k + 1) * LANES)
        flows[rows, :] = pair(-(root_t[:, k : k + 1] * sketch_ref[rows, :].astype(f32)))

    def spread_columns():
        for values, store in ((new_src, srcb), (new_dst, dstb), (new_held, wb)):
            turned = values[...].T
            for k in range(wide_rows):
                rows = slice(k * LANES, (k + 1) * LANES)
                store[rows, :] = jnp.broadcast_to(turned[:, k : k + 1], (LANES, LANES)).astype(store.dtype)
        for k in range(wide_rows):
            cols = slice(k * LANES, (k + 1) * LANES)
            rowf[4:5, cols] = new_src[k : k + 1, :]
            rowf[5:6, cols] = new_dst[k : k + 1, :]
        spread_lists(new_list, 1)
        for ref in (res, dirn, sol, part):
            ref[...] = jnp.zeros(ref.shape, f32)

    def count_up(rows, up_at, low, weights):
        edges = weights.shape[1]
        up = lax.broadcasted_iota(i32, (rows, edges), 0)
        picked = jnp.where(up == up_at, weights, 0.0)
        parts = dot_lanes(jnp.concatenate(split3(picked), axis=0), one_hot(down_rows(low, 0, LANES)))
        return parts[:rows] + parts[rows : 2 * rows] + parts[2 * rows :]

    def degree_of(to):
        return degh.at[to]

    def far_degree():
        got = count_up(-(-peers // 16) * 16, rowf[2:3, :], rowf[3:4, :], wide[0:1, :num_edges])
        for q in range(peers):
            degh[q] = jnp.broadcast_to(got[q : q + 1, :], (8, LANES))
        exchange(at_home, degree_of, dback, deg_sem.at[0], deg_sem.at[1])
        dback[me] = degh[me]

    def spread_lists(lists, row):
        list_t = lists[...].T
        for q in range(peers):
            listb[q * slot : (q + 1) * slot, :] = jnp.broadcast_to(list_t[:, q : q + 1], (LANES, LANES))[:slot]
        for at in range(0, halo_len, LANES):
            listrow[row : row + 1, at : at + LANES] = listb[at : at + LANES, :].T[0:1, :]

    def scatter_rows(at, rows, edges):
        acc[:rows, :] = jnp.zeros((rows, 2 * columns), f32)

        def body(k, _):
            cols = pl.ds(pl.multiple_of(k * ktile, ktile), ktile)
            pick = signed(down_rows(rowf[edges : edges + 1, cols], at, rows), down_rows(rowf[edges + 1 : edges + 2, cols], at, rows))
            acc[:rows, :] += dot(pick, flows[cols, :])
            return 0

        lax.fori_loop(0, num_edges // ktile, body, 0)
        return halves(acc[:rows, :])

    def edge_hots(rows, at, width):
        hots = zip(along_lanes(srcb[rows, :], at, width), along_lanes(dstb[rows, :], at, width))
        return jnp.concatenate([signed(a, b) for a, b in hots], axis=1)

    def gather_near(group, q, tail=False):
        for off in range(0, quarter, etile):
            rows = pl.ds(pl.multiple_of(q * quarter + off, etile), etile)
            base = pl.multiple_of(group * GROUP, GROUP)
            hots = edge_hots(rows, base, GROUP)
            got = part[rows, :] + halves(dot(hots, field[pl.ds(base, GROUP), :]))
            part[rows, :] = got
            if tail:
                flows[rows, :] = pair(got * wb[rows, :])

    def own_degree():
        rows = -(-high // 16) * 16
        got = jnp.zeros((rows, LANES), f32)
        for row in (0, 1):
            at = rowf[row : row + 1, :]
            got += count_up(rows, at // LANES, at % LANES, wide[0:1, :num_edges])
        for q in range(peers):
            list8row[0:1, q * LANES : (q + 1) * LANES] = list8[q : q + 1, :]
            wide[1:2, q * LANES : (q + 1) * LANES] = dback[q, 0:1, :]
        at = list8row[...]
        landing = count_up(rows, jnp.where(at < 0, -1, at // LANES), at % LANES, wide[1:2, : peers * LANES])
        degown[:high, :] = (got + landing)[:high]
        degown[high:, :] = landing[:high]

    def degree_copy(kind, land, src, dst, target):
        return remote(src, dst, degline_sem.at[0, kind], degline_sem.at[1, land], target)

    def degree_sum():
        return degree_copy(0, 0, degown, degouter, inward)

    def degree_part():
        return degree_copy(1, 1, degmine, deginner, inward)

    def degree_total(j):
        return degree_copy(2 + j, 2, degtotal, degtotal, totals_to[j])

    hpiece = even_piece(halo_len, 512)

    def back_of(s, place):
        def halo_of(to):
            return yhalo.at[s, pl.ds(pl.multiple_of(to * slot, 8), slot)]

        return place, halo_of, back.at[s], back_sem.at[0, s], back_sem.at[1, s]

    def send_back(s, place, edges):
        for at in range(0, halo_len, hpiece):
            yhalo[s, at : at + hpiece, :] = scatter_rows(num_rows + at, hpiece, edges)
        if edges == 0:
            pl.semaphore_wait(barrier, greeted)
        exchange(*back_of(s, place))
        back[s, place[0]] = yhalo[s, pl.ds(pl.multiple_of(place[0] * slot, 8), slot), :]

    send_back(0, at_home, 0)

    @pl.when(moves)
    def _():
        for copy in swaps():
            copy.start()

    far_degree()
    spread_lists(list8, 0)

    def piece_rows(k):
        return pl.ds(pl.multiple_of(k * PIECE, PIECE), PIECE)

    def line_copy(s, kind, land, k, src, dst, target):
        rows = piece_rows(k)
        return remote(
            src.at[s, rows], dst.at[s, rows], line_sem.at[0, s, kind, k], line_sem.at[1, s, land, k], target
        )

    def own_rows(s, c, place, edges, size):
        at = pl.multiple_of(c * size, size)
        local = scatter_rows(at, size, edges)

        @pl.when(c == 0)
        def _():
            exchange_wait(*back_of(s, place))
            retb[...] = pair(back[s].reshape(halo_len, columns))

        pick = one_hot(down_rows(listrow[min(edges, 1) : min(edges, 1) + 1, :], at, size))
        own[s, pl.ds(at, size), :] = local + halves(dot(pick, retb[...]))

    def update(s, rows, keep, push, last):
        old = dirn[rows, :]
        residual = res[rows, :] - (groundb[rows, :] * old + total[s, rows, :])
        direction = keep * old + push * invb[rows, :] * residual
        shown = sol[rows, :] + direction
        res[rows, :] = residual
        dirn[rows, :] = direction
        sol[rows, :] = shown
        field[rows, :] = pair(jnp.where(last, shown, direction))

    def pick_group(s, group):
        base = pl.multiple_of(group * GROUP, GROUP)
        for at in range(0, halo_len, hpiece):
            spread = listb[at : at + hpiece, :].astype(jnp.int16)
            hots = jnp.concatenate([one_hot(m) for m in along_lanes(spread, base, GROUP)], axis=1)
            got = halves(dot(hots, field[pl.ds(base, GROUP), :]))
            listed[s, at : at + hpiece, :] = jnp.where(group == 0, got, listed[s, at : at + hpiece, :] + got)

    def sum_at_home(keep, push, last):
        def to_inward(k):
            return line_copy(0, 0, 0, k, own, outer, inward)

        def part_inward(k):
            return line_copy(0, 1, 1, k, mine, inner, inward)

        def give_total(k, j):
            return line_copy(0, 2 + j, 2, k, total, total, totals_to[j])

        def pass_partial(k):
            rows = piece_rows(k)
            to_inward(k).wait_recv()
            mine[0, rows, :] = own[0, rows, :] + outer[0, rows, :]
            part_inward(k).start()

        sends = jnp.logical_or(u == 0, u == 3)

        def send_group(c):
            for j in range(HOME_GROUP // PIECE):
                to_inward(c * (HOME_GROUP // PIECE) + j).start()

        def group_rows(c, _):
            own_rows(0, c, at_home, 0, HOME_GROUP)

            @pl.when(u == 3)
            def _():
                send_group(c)

            @pl.when(jnp.logical_and(u == 0, c >= HOLD))
            def _():
                send_group(c - HOLD)

            @pl.when(c == 0)
            def _():
                exchange_wait(at_home, degree_of, dback, deg_sem.at[0], deg_sem.at[1])
                own_degree()

                @pl.when(sends)
                def _():
                    degree_sum().start()

            @pl.when(jnp.logical_and(u == 2, c == home_groups - 2))
            def _():
                degree_sum().wait_recv()
                degmine[...] = degown[...] + degouter[...]
                degree_part().start()
                for k in range(LAG // 2):
                    pass_partial(k)

            @pl.when(c == home_groups - 2)
            def _():
                @pl.when(moves)
                def _():
                    for copy in swaps():
                        copy.wait()

                spread_columns()

            @pl.when(jnp.logical_and(u == 2, c == home_groups - 1))
            def _():
                for k in range(LAG // 2, LAG):
                    pass_partial(k)

            return 0

        lax.fori_loop(0, home_groups, group_rows, 0)

        @pl.when(u == 0)
        def _():
            for c in range(home_groups - HOLD, home_groups):
                send_group(c)

        @pl.when(u == 1)
        def _():
            degree_sum().wait_recv()
            degree_part().wait_recv()
            degtotal[...] = (degown[...] + degouter[...]) + deginner[...]
            for j in range(3):
                degree_total(j).start()

        @pl.when(u != 1)
        def _():
            degree_total(0).wait_recv()

        inverse_t = (1.0 / (degtotal[:high, :] + new_ground[...])).T
        held_t = (degtotal[high:, :] + new_ground[...]).T
        for j in range(high):
            rows = slice(j * LANES, (j + 1) * LANES)
            invb[rows, :] = jnp.broadcast_to(inverse_t[:, j : j + 1], (LANES, LANES))
            groundb[rows, :] = jnp.broadcast_to(held_t[:, j : j + 1], (LANES, LANES))

        def step(k, _):
            rows = piece_rows(k)

            @pl.when(jnp.logical_and(u == 2, k + LAG < count))
            def _():
                pass_partial(k + LAG)

            @pl.when(u == 1)
            def _():
                to_inward(k).wait_recv()
                part_inward(k).wait_recv()
                total[0, rows, :] = (own[0, rows, :] + outer[0, rows, :]) + inner[0, rows, :]
                for j in range(3):
                    give_total(k, j).start()

            @pl.when(u != 1)
            def _():
                give_total(k, 0).wait_recv()

            update(0, rows, keep, push, last)
            group, j = k // per, lax.rem(k, per)

            @pl.when(j == per - 1)
            def _():
                pick_group(0, group)

            @pl.when(jnp.logical_and(group > 0, k < count - per // 2))
            def _():
                gather_near(group - 1, j)

            return 0

        lax.fori_loop(0, count, step, 0)

        def line_done(k, _):
            @pl.when(sends)
            def _():
                to_inward(k).wait_send()

            @pl.when(u == 2)
            def _():
                part_inward(k).wait_send()

            @pl.when(u == 1)
            def _():
                for j in range(3):
                    give_total(k, j).wait_send()

            return 0

        lax.fori_loop(0, count, line_done, 0)

        @pl.when(sends)
        def _():
            degree_sum().wait_send()

        @pl.when(u == 2)
        def _():
            degree_part().wait_send()

        @pl.when(u == 1)
        def _():
            for j in range(3):
                degree_total(j).wait_send()

    def show(m, held_in):
        rows = pl.ds(pl.multiple_of(m * 2 * PIECE, 2 * PIECE), 2 * PIECE)
        return remote(held_in.at[rows], sol_in.at[rows], sol_sem.at[0, m], sol_sem.at[1, m], outward)

    def first_show(m):
        return show(m, sol)

    def next_show(m):
        return show(m, sol_in)

    def forward(m):
        first_show(m).wait_recv()
        next_show(m).start()

    def sum_at_host(s, keep, push, last):
        def lend(k):
            return line_copy(s, 0, 0, k, own, outer, other_core)

        def cross(k):
            return line_copy(s, 1, 1, k, mine, inner, across)

        def share(k):
            return line_copy(s, 2, 2, k, total, total, other_core)

        def pair_sum(c):
            for j in range(host_pairs):
                k = (c * host_pairs + j) * 2 + core
                rows = piece_rows(k)
                lend(k).wait_recv()
                mine[s, rows, :] = own[s, rows, :] + outer[s, rows, :]
                cross(k).start()

        def group_rows(c, _):
            own_rows(s, c, at_host, 4, HOST_GROUP)
            for j in range(host_pairs):
                lend((c * host_pairs + j) * 2 + 1 - core).start()

            @pl.when(c > 0)
            def _():
                pair_sum(c - 1)

            return 0

        lax.fori_loop(0, host_groups, group_rows, 0)
        pair_sum(host_groups - 1)

        def step(m, _):
            k = 2 * m + core
            rows = piece_rows(k)
            cross(k).wait_recv()
            total[s, rows, :] = mine[s, rows, :] + inner[s, rows, :]
            share(k).start()
            group, j = m // (per // 2), lax.rem(m, per // 2)

            @pl.when(jnp.logical_and(group > 0, m < count // 2 - 1))
            def _():
                gather_near(group - 1, 2 * j)
                gather_near(group - 1, 2 * j + 1)

            share(2 * m + 1 - core).wait_recv()
            update(s, pl.ds(pl.multiple_of(m * 2 * PIECE, 2 * PIECE), 2 * PIECE), keep, push, last)

            @pl.when(jnp.logical_and(last, u == 1))
            def _():
                first_show(m).start()

            @pl.when(jnp.logical_and(jnp.logical_and(last, u == 2), m >= LEAD))
            def _():
                forward(m - LEAD)

            @pl.when(j == per // 2 - 1)
            def _():
                pick_group(s, group)

            return 0

        lax.fori_loop(0, count // 2, step, 0)

        def sent(m, _):
            lend(2 * m + 1 - core).wait_send()
            cross(2 * m + core).wait_send()
            share(2 * m + core).wait_send()
            return 0

        lax.fori_loop(0, count // 2, sent, 0)

    def stage(s, _):
        begin, last = s == 0, s == ITERS - 1
        keep, push = jnp.float32(0.0), jnp.float32(first)
        for at, (k_coef, p_coef) in enumerate(pairs):
            keep = jnp.where(s == at + 1, jnp.float32(k_coef), keep)
            push = jnp.where(s == at + 1, jnp.float32(p_coef), push)

        @pl.when(begin)
        def _():
            sum_at_home(keep, push, last)

        @pl.when(jnp.logical_not(begin))
        def _():
            sum_at_host(s, keep, push, last)

        def listed_of(to):
            return listed.at[s, pl.ds(pl.multiple_of(to * slot, 8), slot)]

        land_args = (at_host, listed_of, landed.at[s], land_sem.at[0, s], land_sem.at[1, s])
        exchange(*land_args)
        landed[s, block] = listed[s, pl.ds(pl.multiple_of(block * slot, 8), slot), :]

        def near_left(q, _):
            gather_near(groups - 2, q)
            return 0

        lax.fori_loop(per // 2, per, near_left, 0)

        def near_tail(q, _):
            gather_near(groups - 1, q, True)
            return 0

        lax.fori_loop(0, 4, near_tail, 0)

        @pl.when(jnp.logical_not(last))
        def _():
            send_back(s + 1, at_host, 4)

        @pl.when(jnp.logical_and(last, u == 2))
        def _():
            for m in range(count // 2 - LEAD, count // 2):
                forward(m)

        exchange_wait(*land_args)
        field[num_rows:, :] = pair(landed[s].reshape(halo_len, columns))

        def gather_far(k):
            rows = pl.ds(pl.multiple_of(k * etile, etile), etile)
            gap = part[rows, :] + halves(dot(edge_hots(rows, num_rows, halo_len), field[num_rows:, :]))
            part[rows, :] = jnp.zeros(gap.shape, f32)
            return rows, gap

        @pl.when(jnp.logical_not(last))
        def _():
            def make_flows(k, _):
                rows, gap = gather_far(k)
                flows[rows, :] = pair(gap * wb[rows, :])
                return 0

            lax.fori_loop(0, num_edges // etile, make_flows, 0)

        @pl.when(last)
        def _():
            def make_gaps(k, _):
                rows, gap = gather_far(k)
                square = gap * gap
                for i in range(etile // LANES):
                    turned = square[i * LANES : (i + 1) * LANES, :].T
                    row = pl.ds(k * (etile // LANES) + i, 1)
                    gaps[row, :] = jnp.sum(turned, axis=0, keepdims=True)
                return 0

            lax.fori_loop(0, num_edges // etile, make_gaps, 0)

        return 0

    lax.fori_loop(0, ITERS, stage, 0)

    def gaps_home():
        return remote(gaps, gaps_in, swap_sem.at[0, 5], swap_sem.at[1, 5], swap_with)

    @pl.when(stays)
    def _():
        out_ref[...] = sol[...]
        gap_ref[...] = mask[...] * gaps[...] / columns

    @pl.when(moves)
    def _():
        gaps_home().start()

    @pl.when(u == 3)
    def _():
        for m in range(count // 2):
            first_show(m).wait_recv()

    @pl.when(jnp.logical_or(u == 1, u == 2))
    def _():
        for m in range(count // 2):
            first_show(m).wait_send()

    @pl.when(moves)
    def _():
        out_ref[...] = sol_in[...]
        gaps_home().wait()
        gap_ref[...] = mask[...] * gaps_in[...] / columns


def local(sketch_cols, edge_weight, ground, src_local, dst_index, send_rows, edge_count):
    peers = lax.axis_size("vtx")
    num_rows, num_edges = ground.shape[0], edge_weight.shape[0]
    slot, columns = send_rows.shape[2], sketch_cols.shape[1]
    halo_len, high, wide_rows = peers * slot, num_rows // LANES, num_edges // LANES
    count = num_rows // PIECE
    f32, bf16, i32, i16 = jnp.float32, jnp.bfloat16, jnp.int32, jnp.int16
    vmem, dma = pltpu.VMEM, pltpu.SemaphoreType.DMA
    peers8 = -(-peers // 8) * 8
    halo = vmem((ITERS, peers, slot, columns), f32)
    flat_halo = vmem((ITERS, halo_len, columns), f32)
    rows_f32 = vmem((num_rows, columns), f32)
    line = vmem((ITERS, num_rows, columns), f32)
    small = vmem((2 * high, LANES), f32)
    spread = vmem((num_edges, LANES), i16)
    wide_f32 = vmem((wide_rows, LANES), f32)
    scratch = [
        vmem((8, num_edges), i32), spread, spread,
        vmem((8, max(num_edges, peers * LANES)), f32), vmem((num_edges, LANES), f32),
        vmem((halo_len, LANES), i32), vmem((2, halo_len), i32),
        rows_f32, rows_f32, rows_f32, rows_f32, rows_f32,
        vmem((num_rows + halo_len, 2 * columns), bf16), vmem((num_edges, columns), f32),
        vmem((max(512, GROUP, HOST_GROUP, HOME_GROUP), 2 * columns), f32), vmem((halo_len, 2 * columns), bf16),
        vmem((num_edges, 2 * columns), bf16), line, line, line, line, line,
        flat_halo, halo, flat_halo, halo,
        vmem((wide_rows, LANES), f32), vmem((peers8, LANES), i32),
        vmem((1, peers * LANES), i32),
        small, small, small, small, small, vmem((peers, 8, LANES), f32), vmem((peers, 8, LANES), f32),
        vmem((wide_rows, LANES), i32), vmem((wide_rows, LANES), i32), wide_f32, wide_f32,
        vmem((peers8, LANES), i32), vmem((high, LANES), f32), wide_f32, wide_f32, rows_f32,
        dma((2, ITERS, peers)), dma((2, ITERS, peers)), dma((2, peers)), dma((2, ITERS, 5, count)), dma((2, 5)),
        dma((2, 6)), dma((2, count // 2)),
    ]
    in_vmem = pl.BlockSpec(memory_space=pltpu.VMEM)
    solution, gaps = pl.pallas_call(
        functools.partial(kernel, peers),
        in_specs=[in_vmem] * 6 + [pl.BlockSpec(memory_space=pltpu.SMEM)],
        out_specs=[in_vmem] * 2,
        out_shape=[pltpu.VMEM((num_rows, columns), f32), pltpu.VMEM((wide_rows, LANES), f32)],
        scratch_shapes=scratch,
        compiler_params=pltpu.CompilerParams(collective_id=0, has_side_effects=True, vmem_limit_bytes=VMEM_LIMIT),
        name="sketch",
    )(
        sketch_cols, edge_weight.reshape(wide_rows, LANES), ground.reshape(high, LANES),
        src_local.reshape(wide_rows, LANES), dst_index.reshape(wide_rows, LANES), send_rows[0], edge_count,
    )
    return solution, gaps.reshape(-1)


def solution(mesh):
    in_specs = (
        P(("vtx", "edg"), None),
        P(("vtx", "edg")),
        P("vtx"),
        P(("vtx", "edg")),
        P(("vtx", "edg")),
        P(("vtx", "edg"), None, None),
        P(("vtx", "edg")),
    )
    out_specs = (P("vtx", None), P(("vtx", "edg")))
    return jax.shard_map(local, mesh=mesh, in_specs=in_specs, out_specs=out_specs, check_vma=False)
```
